512 devices in a mesh: seq: 32 (over z, y_lo), head: 16 (over y_hi, x, core).
Axes of the slice: x: 4, y: 4 (y_hi: 2, y_lo: 2; y = y_hi * 2 + y_lo), z: 16, core: 2. Of those that a mesh axis runs over, the one named last changes fastest.
Arguments:
- byte_states: bfloat16 [24576, 1280], P('seq', 'head'), may hold values from -19 to 19
- patch_ids: int32 [24576], P('seq'), may hold values from 0 to 3071, never falling along the last dimension, each value on 1 to 16 neighbouring positions
- slot_patch: int32 [3072], replicated, may hold values from 0 to 3071, each once
- pool_gain: float32 [1280], replicated, may hold values from 0.25 to 1.75
- w_in: bfloat16 [1280, 4096], P('seq', 'head'), may hold values from -0.16910264 to 0.16910264
- attn_gain: float32 [4096], replicated, may hold values from 0.25 to 1.75
- w_qkv: bfloat16 [4096, 3, 4096], P('seq', None, 'head'), may hold values from -0.5105401 to 0.5105401
- w_out: bfloat16 [4096, 4096], P('head'), may hold values from -0.09375 to 0.09375
- w_down: bfloat16 [4096, 1280], P('head', 'seq'), may hold values from -0.34375 to 0.34375
Outputs:
- patch_out: bfloat16 [3072, 4096], P('seq', 'head')
- byte_out: bfloat16 [24576, 1280], P('seq', 'head')
The draws below stay inside these ranges and needn't reach their ends.
Inputs may be any that keep to these rules, and one draw needn't show every extreme that they name: patch_ids never falls along the bytes; each of the 3072 patches holds 1 to 16 consecutive bytes, and some patch exactly 16. `slot_patch`: every patch number appears once; slot r belongs to segment r // 96.
All inputs are finite; a program needn't handle non-finite values.
Results may differ from the reference program's by a relative error of at most 0.015.
Values may be sent and summed in bfloat16 or wider, within the bound.
No kernel may reach another device: no remote copies, remote signals or barrier semaphores. Data moves between devices by JAX's collectives and lax.ppermute only.
A program may use at most 64 MiB of HBM per device.

```python
import math
from functools import partial
import jax
import jax.numpy as jnp
import numpy as np
from jax import lax

BYTE_WIDTH = 1280
MODEL_WIDTH = 4096
HEAD_SIZE = 128
LONGEST = 16
WINDOW = 8
BYTES_DEV = 768
BYTES = 24576
PATCHES = 3072
HEADS = 32
N_SEQ = 32
N_HEAD = 16


def input_matrix(key):
    return jax.random.truncated_normal(jax.random.fold_in(key, 7101), -6.0, 6.0, (BYTE_WIDTH, MODEL_WIDTH), jnp.float32) / math.sqrt(BYTE_WIDTH)


def draw_w_in(key, part):
    return input_matrix(key).astype(jnp.bfloat16)


def draw_w_down(key, part):
    spread_part = jax.random.truncated_normal(jax.random.fold_in(key, 7102), -6.0, 6.0, (MODEL_WIDTH, BYTE_WIDTH), jnp.float32) / math.sqrt(MODEL_WIDTH)
    return spread_part.astype(jnp.bfloat16)


def draw_w_qkv(key, part):
    normal_part = jax.random.truncated_normal(jax.random.fold_in(key, 7201), -6.0, 6.0, (MODEL_WIDTH, 3, HEADS * HEAD_SIZE), jnp.float32) / math.sqrt(MODEL_WIDTH)
    ranking = jax.random.permutation(jax.random.fold_in(key, 7202), HEADS)
    strong_count = max(1, HEADS // 4)
    levels = jnp.clip(strong_count - 1 - ranking, 0, strong_count - 1).astype(jnp.float32)
    strength = 330.0 * (1.0 / 3.0) ** (levels / max(strong_count - 1, 1))
    factor = jnp.repeat(jnp.sqrt(strength / math.sqrt(HEAD_SIZE)), HEAD_SIZE)
    strong = jnp.repeat(ranking < strong_count, HEAD_SIZE)
    queries = normal_part[:, 0, :]
    aligned = factor[None, :] * queries
    query_part = jnp.where(strong[None, :], aligned, queries)
    key_part = jnp.where(strong[None, :], aligned, normal_part[:, 1, :])
    return jnp.stack([query_part, key_part, normal_part[:, 2, :]], axis=1).astype(jnp.bfloat16)


def slow_field(key):
    coeffs = jax.random.normal(jax.random.fold_in(key, 7304), (3,), jnp.float32)
    phases = jax.random.uniform(jax.random.fold_in(key, 7305), (3,), jnp.float32, 0.0, 2.0 * math.pi)
    position = jnp.arange(BYTES, dtype=jnp.float32) / BYTES
    rates = jnp.arange(1, 4, dtype=jnp.float32)
    field = jnp.sum(coeffs[:, None] * jnp.sin(2.0 * math.pi * rates[:, None] * position[None, :] + phases[:, None]), axis=0)
    return field / (jnp.max(jnp.abs(field)) + 1e-06)


def draw_byte_states(key, part):
    rough_part = jax.random.truncated_normal(jax.random.fold_in(key, 7301), -6.0, 6.0, (BYTES, BYTE_WIDTH), jnp.float32)
    common = jax.random.truncated_normal(jax.random.fold_in(key, 7302), -2.5, 2.5, (BYTE_WIDTH,), jnp.float32)
    field = slow_field(key)
    return (2.0 * field[:, None] * common[None, :] + rough_part).astype(jnp.bfloat16)


def level_of(rng, dims, cuts, smallest, top_value):
    level = 1.0
    for dim, shards_of in cuts:
        draws = jax.random.uniform(jax.random.fold_in(jax.random.fold_in(rng, 6), dim), (shards_of,), jnp.float32, smallest / len(cuts), top_value / len(cuts))
        level = level * jnp.repeat(jnp.exp(draws), dims[dim] // shards_of).reshape((-1,) + (1,) * (len(dims) - 1 - dim))
    return level


def split_up(number_of, total, most, lean):
    weights = [(1 << 20) // math.isqrt(grade ** lean) + 1 for grade in range(2, number_of + 1)]
    spare, counts = total - most - (number_of - 1), [1] * (number_of - 1)
    while spare > 0:
        candidates = [i for i in range(number_of - 1) if counts[i] < most]
        whole, left = sum([weights[i] for i in candidates]), spare
        for i in candidates:
            extra = min(most - counts[i], max(1, left * weights[i] // whole), spare)
            counts[i] = counts[i] + extra
            spare = spare - extra
    return np.array([most] + counts)


def uneven(key, amount, total, bound, skew):
    if amount == 2:
        one = jax.random.randint(key, (), max(1, total - bound), min(bound, total - 1) + 1)
        return jnp.stack([one, total - one])
    sizes = jnp.asarray(split_up(amount, total, bound, skew), jnp.int32)
    couples = (amount - 1) // 2
    source_of, receiver = sizes[1:1 + 2 * couples:2], sizes[2:2 + 2 * couples:2]
    margin = jnp.minimum(source_of - 1, bound - receiver)
    passed = jax.random.randint(jax.random.fold_in(key, 1), (couples,), 0, 1 << 20) % (margin + 1)
    sizes = sizes.at[1:1 + 2 * couples:2].set(source_of - passed).at[2:2 + 2 * couples:2].set(receiver + passed)
    return sizes[jax.random.permutation(jax.random.fold_in(key, 2), amount)]


def normal_values(own_key, shape, scale, most, cuts=(), kind=jnp.bfloat16):
    values = jax.random.normal(own_key, shape, jnp.float32) * scale
    if len(cuts) > 0:
        values = level_of(own_key, shape, cuts, -0.22, 0.18) * values
    return jnp.clip(values, min=-most, max=most).astype(kind)


def setup_inputs(seed: int = 0) -> dict:
    key_list = jax.random.split(jax.random.key(seed), 10)
    return {
        "byte_states": draw_byte_states(jax.random.fold_in(key_list[9], 71), 0),
        "patch_ids": jnp.searchsorted(jnp.cumsum(uneven(key_list[1], PATCHES, BYTES, LONGEST, 2)), jnp.arange(BYTES), side="right").astype(jnp.int32),
        "slot_patch": jax.random.permutation(key_list[2], PATCHES).astype(jnp.int32),
        "pool_gain": jnp.clip(1.0 + 0.15 * jax.random.normal(key_list[3], (BYTE_WIDTH,), jnp.float32), 0.25, 1.75),
        "w_in": draw_w_in(jax.random.fold_in(key_list[9], 71), 0),
        "attn_gain": jnp.clip(1.0 + 0.15 * jax.random.normal(key_list[5], (MODEL_WIDTH,), jnp.float32), 0.25, 1.75),
        "w_qkv": draw_w_qkv(jax.random.fold_in(key_list[9], 71), 0),
        "w_out": normal_values(key_list[7], (HEADS * HEAD_SIZE, MODEL_WIDTH), (HEADS * HEAD_SIZE) ** -0.5, 0.09375, ((0, 16),)),
        "w_down": draw_w_down(jax.random.fold_in(key_list[9], 71), 0),
    }


EPSILON = 1e-05

def rms_scale(values, gain):
    wide = values.astype(jnp.float32)
    return wide * lax.rsqrt(lax.optimization_barrier(jnp.mean(wide * wide, axis=-1, keepdims=True)) + EPSILON) * gain

def global_head(operands):
    queries, keys, values = operands
    scores = jnp.dot(queries, keys.T, preferred_element_type=jnp.float32) / math.sqrt(HEAD_SIZE)
    order = jnp.arange(PATCHES, dtype=jnp.int32)
    allowed = order[:, None] >= order[None, :]
    scores = jnp.where(allowed, scores, -jnp.inf)
    peak = lax.optimization_barrier(jnp.max(scores, axis=1, keepdims=True))
    weights = jnp.exp(scores - peak)
    total = lax.optimization_barrier(jnp.sum(weights, axis=1, keepdims=True))
    mixed = jnp.dot(weights.astype(jnp.bfloat16), values, preferred_element_type=jnp.float32)
    return (mixed / total).astype(jnp.bfloat16)

def cross_block(patch_states, operands):
    states, labels = operands
    heads = N_HEAD
    size = BYTE_WIDTH // N_HEAD
    reach = labels[:, None] - jnp.arange(WINDOW, dtype=jnp.int32)[None, :]
    valid = reach >= 0
    rows = patch_states[jnp.maximum(reach, 0).astype(jnp.int32)]
    queries = states.astype(jnp.float32).reshape(BYTES_DEV, heads, size)
    keys = rows.astype(jnp.float32).reshape(BYTES_DEV, WINDOW, heads, size)
    scores = jnp.einsum('bhc,bwhc->bhw', queries, keys, precision=lax.Precision.HIGHEST) / math.sqrt(size)
    scores = jnp.where(valid[:, None, :], scores, -jnp.inf)
    peak = lax.optimization_barrier(jnp.max(scores, axis=-1, keepdims=True))
    weights = jnp.exp(scores - peak)
    total = lax.optimization_barrier(jnp.sum(weights, axis=-1, keepdims=True))
    rounded = lax.optimization_barrier(weights.astype(jnp.bfloat16)).astype(jnp.float32)
    mixed = jnp.einsum('bhw,bwhc->bhc', rounded, keys, precision=lax.Precision.HIGHEST) / total
    return (states.astype(jnp.float32) + mixed.reshape(BYTES_DEV, BYTE_WIDTH)).astype(jnp.bfloat16)

def reference(byte_states, patch_ids, slot_patch, pool_gain, w_in, attn_gain, w_qkv, w_out, w_down):
    pooled = jax.ops.segment_sum(byte_states.astype(jnp.float32), patch_ids, num_segments=PATCHES).astype(jnp.bfloat16)
    normed = rms_scale(pooled, pool_gain).astype(jnp.bfloat16)
    embed = jnp.dot(normed, w_in, preferred_element_type=jnp.float32).astype(jnp.bfloat16)
    attn_in = rms_scale(embed, attn_gain).astype(jnp.bfloat16)
    width = HEADS * HEAD_SIZE
    projected = jnp.dot(attn_in, w_qkv.reshape(MODEL_WIDTH, 3 * width), preferred_element_type=jnp.float32).astype(jnp.bfloat16)
    split = projected.reshape(PATCHES, 3, HEADS, HEAD_SIZE).transpose(1, 2, 0, 3)
    attended = lax.map(global_head, (split[0], split[1], split[2]))
    attended = attended.transpose(1, 0, 2).reshape(PATCHES, width)
    stream = (embed.astype(jnp.float32) + jnp.dot(attended, w_out, preferred_element_type=jnp.float32)).astype(jnp.bfloat16)
    patch_out = stream[slot_patch]
    patch_states = jnp.dot(stream, w_down, preferred_element_type=jnp.float32).astype(jnp.bfloat16)
    blocks = lax.map(partial(cross_block, patch_states), (byte_states.reshape(N_SEQ, BYTES_DEV, BYTE_WIDTH), patch_ids.reshape(N_SEQ, BYTES_DEV)))
    byte_out = blocks.reshape(BYTES, BYTE_WIDTH)
    return (patch_out, byte_out)
```

```python
import functools
import math

import jax
import jax.numpy as jnp
from jax import lax
from jax.experimental import pallas as pl
from jax.experimental.pallas import tpu as pltpu
from jax.sharding import Mesh
from jax.sharding import PartitionSpec as P


HEAD_SIZE = 128
WINDOW = 8
LONGEST = 16
ZL = ("zm", "zp")
Z = ("zh", "zm", "zp")
SEQ = ("zh", "zm", "zp", "yl")
SKIP = ("zh", "zm", "yl")
PLANE = ("yl", "yh", "x")
HEAD = ("yh", "x", "c")
EPSILON = 1e-05
FLOOR_SCORE = -1e30
BF = jnp.bfloat16
F32 = jnp.float32
MAIN = 64
LANES = 128


VMEM = pl.BlockSpec(memory_space=pltpu.VMEM)
SMEM = pl.BlockSpec(memory_space=pltpu.SMEM)


def local_call(kernel, out, inputs, scratch=(), scalars=0, flops=10**8, moved=10**6):
    specs = [SMEM] * scalars + [VMEM] * (len(inputs) - scalars)
    many = isinstance(out, (list, tuple))
    return pl.pallas_call(
        kernel,
        out_shape=out,
        in_specs=specs,
        out_specs=[VMEM] * len(out) if many else VMEM,
        scratch_shapes=list(scratch),
        compiler_params=pltpu.CompilerParams(vmem_limit_bytes=48 << 20),
        cost_estimate=pl.CostEstimate(flops=flops, bytes_accessed=moved, transcendentals=0),
    )(*inputs)


def matmul(a, b):
    return lax.dot_general(a, b, (((1,), (0,)), ((), ())), preferred_element_type=F32)


def matmul_t(a, b):
    return lax.dot_general(a, b, (((1,), (1,)), ((), ())), preferred_element_type=F32)


def pool_kernel(flip, info, slots, ids, rows, out):
    blocks, packed_rows, _ = out.shape
    count = slots.shape[0] // (2 * blocks)
    half = count // 2
    group = packed_rows - half
    blank = jnp.zeros((group, LANES - group * (count // group)), F32)
    side = 1 - info[1] if flip else info[1]

    def step(i, unused):
        at = pl.multiple_of((2 * i + side) * count, count)
        match = jnp.where(slots[pl.ds(at, count), :] == ids[...], 1.0, 0.0).astype(BF)
        part = matmul_t(match, rows[...])
        out[i, 0:half, 0:MAIN] = part[0:half, 0:MAIN].astype(BF)
        out[i, 0:half, MAIN:LANES] = part[half:count, 0:MAIN].astype(BF)
        rest = [part[group * g : group * (g + 1), MAIN:] for g in range(count // group)]
        out[i, half:packed_rows, :] = jnp.concatenate(rest + [blank], axis=1).astype(BF)
        return unused

    lax.fori_loop(0, blocks, step, 0, unroll=4)


def sum_kernel(arrived, out):
    total = jnp.zeros(arrived.shape[1:], F32)
    for i in range(arrived.shape[0]):
        total = total + arrived[i].astype(F32)
    held = total.astype(BF)
    for i in range(out.shape[0]):
        out[i] = held


def embed_kernel(info, own, other, gain, w_in, out, keep):
    planes = own.shape[0] // 2
    count, size = keep.shape[1:]
    each = count // 2
    half = each // 2
    spare = size - MAIN
    group = own.shape[1] - half
    square = jnp.zeros((count, 1), F32)
    for side, source in ((0, own), (1, other)):
        for p in range(planes):
            two = [source[y * planes + p].astype(F32) for y in range(2)]
            main = [v[0:half, at : at + MAIN] for v in two for at in (0, MAIN)]
            main = jnp.concatenate(main, axis=0)
            rest = [
                v[half:, spare * g : spare * (g + 1)] for v in two for g in range(each // group)
            ]
            rest = jnp.concatenate(rest, axis=0)
            keep[side * planes + p, :, 0:MAIN] = main
            keep[side * planes + p, :, MAIN:size] = rest
            square = square + jnp.sum(main * main, axis=1, keepdims=True)
            square = square + jnp.sum(rest * rest, axis=1, keepdims=True)
    scale = lax.rsqrt(square / (2 * planes * size) + EPSILON)
    total = jnp.zeros(out.shape[1:], F32)
    for side in range(2):
        core = info[0] if side == 0 else 1 - info[0]
        for p in range(planes):
            h = 2 * p + core
            normed = keep[side * planes + p] * scale * gain[pl.ds(h, 1), :]
            at = pl.multiple_of(h * size, 16)
            total = total + matmul(normed.astype(BF), w_in[pl.ds(at, size), :])
    held = total.astype(BF)
    for i in range(out.shape[0]):
        out[i] = held


def project_kernel(info, own, other, gain, weights, queries, kv, down):
    planes = own.shape[0] // 2
    count, width = own.shape[1:]
    size = 2 * width
    columns = 3 * HEAD_SIZE
    square = jnp.zeros((count, width), F32)
    for source in (own, other):
        for b in range(2 * planes):
            wide = source[b].astype(F32)
            square = square + wide * wide
    square = jnp.sum(square, axis=1, keepdims=True)
    scale = lax.rsqrt(square / (2 * planes * size) + EPSILON)
    total = jnp.zeros((count, columns), F32)
    for side, source in ((0, own), (1, other)):
        core = info[0] if side == 0 else 1 - info[0]
        for p in range(planes):
            h = 2 * p + core
            both = jnp.concatenate([source[p], source[planes + p]], axis=1).astype(F32)
            attn_in = both * scale * gain[pl.ds(h, 1), :]
            at = pl.multiple_of(h * size, size)
            total = total + matmul(attn_in.astype(BF), weights[pl.ds(at, size), 0:columns])
    queries[...] = total[:, 0:HEAD_SIZE].astype(BF)
    held = total[:, HEAD_SIZE:].astype(BF)
    for i in range(kv.shape[0]):
        kv[i] = held
    down[...] = weights[:, columns:]


def attend_kernel(info, queries, slots, labels, *rest):
    pieces, keep, send, scores, held = rest[:-4], rest[-4], rest[-3], rest[-2], rest[-1]
    query = queries[...]
    own = pl.multiple_of(info[4] * query.shape[0], query.shape[0])
    mine = slots[pl.ds(own, query.shape[0]), :]
    peak = jnp.full((query.shape[0], 1), FLOOR_SCORE, F32)
    turns = ((0, 0), (3, 0), (1, 0), (2, 0), (2, labels.shape[1] // 2))
    start = 0
    for piece, (turn, at) in zip(pieces, turns):
        size = piece.shape[0]
        here = labels[pl.ds((info[3] + turn) % 4, 1), at : at + size]
        part = matmul_t(query, piece[:, 0:HEAD_SIZE]) * (1.0 / math.sqrt(HEAD_SIZE))
        part = jnp.where(here <= mine, part, FLOOR_SCORE)
        scores[:, start : start + size] = part
        peak = jnp.maximum(peak, jnp.max(part, axis=1, keepdims=True))
        start += size
    total = jnp.zeros_like(peak)
    mixed = jnp.zeros(query.shape, F32)
    start = 0
    for piece in pieces:
        size = piece.shape[0]
        weights = jnp.exp(scores[:, start : start + size] - peak)
        total = total + jnp.sum(weights, axis=1, keepdims=True)
        mixed = mixed + matmul(weights.astype(BF), piece[:, HEAD_SIZE:])
        start += size
    held[...] = mixed / total
    count = keep.shape[0]
    at = pl.multiple_of(info[1] * count, count)
    keep[...] = held[pl.ds(at, count), :].astype(BF)
    at = pl.multiple_of((1 - info[1]) * count, count)
    send[...] = held[pl.ds(at, count), :].astype(BF)


def out_kernel(info, kept, came, w_out, out):
    mine = kept[...]
    theirs = came[...]
    width = out.shape[2]
    at = pl.multiple_of(info[1] * HEAD_SIZE, HEAD_SIZE)
    other = pl.multiple_of((1 - info[1]) * HEAD_SIZE, HEAD_SIZE)
    for h in range(out.shape[0]):
        cols = slice(h * width, (h + 1) * width)
        part = matmul(mine, w_out[pl.ds(at, HEAD_SIZE), cols])
        part = part + matmul(theirs, w_out[pl.ds(other, HEAD_SIZE), cols])
        out[h] = part.astype(BF)


def down_kernel(info, arrived, embed, w_down, stream, out):
    count, width = stream.shape
    half = count // 2
    planes = embed.shape[0] // 2
    size = MAIN + LONGEST
    at = pl.multiple_of(info[1] * count, count)
    low = embed[info[2], pl.ds(at, count), :]
    high = embed[planes + info[2], pl.ds(at, count), :]
    total = jnp.concatenate([low, high], axis=1).astype(F32)
    added = jnp.zeros(total.shape, F32)
    for h in range(arrived.shape[0]):
        added = added + arrived[h].astype(F32)
    held = (total + added).astype(BF)
    stream[...] = held
    group = out.shape[1] - half
    blank = jnp.zeros((group, LANES - LONGEST * (count // group)), F32)
    for h in range(out.shape[0]):
        part = matmul(held, w_down[h * width : (h + 1) * width, :])
        out[h, 0:half, 0:MAIN] = part[0:half, 0:MAIN].astype(BF)
        out[h, 0:half, MAIN:LANES] = part[half:, 0:MAIN].astype(BF)
        rest = [part[group * g : group * (g + 1), MAIN:size] for g in range(count // group)]
        out[h, half:, :] = jnp.concatenate(rest + [blank], axis=1).astype(BF)


def pick_rows(base, labels_main, labels_rest, states, main, rest, put):
    groups = labels_rest.shape[0]
    half = groups * LONGEST // 2
    for i in range(states.shape[0]):
        main[i * half : (i + 1) * half, :] = states[i, 0:half, :]
        rest[i * LONGEST : (i + 1) * LONGEST, :] = states[i, half:, :]
    step = LANES

    def hot(at, label):
        wanted = base + at + lax.broadcasted_iota(jnp.int32, (step, label.shape[1]), 0)
        return jnp.where(wanted == label, 1.0, 0.0).astype(BF)

    def pick(i, unused):
        at = pl.multiple_of(i * step, step)
        low = matmul(hot(at, labels_main[0:1, :]), main[...])
        high = matmul(hot(at, labels_main[1:2, :]), main[...])
        tail = jnp.zeros((step, LONGEST), F32)
        for g in range(groups):
            here = matmul(hot(at, labels_rest[g : g + 1, :]), rest[...])
            tail = tail + here[:, g * LONGEST : (g + 1) * LONGEST]
        put(at, low[:, 0:MAIN] + high[:, MAIN:LANES], tail)
        return unused

    return pick


def near_kernel(info, labels_main, labels_rest, states, out, main, rest):
    group = info[5]

    def put(at, low, tail):
        blank = jnp.zeros((LANES, LANES - MAIN - LONGEST), F32)
        out[pl.ds(at, LANES), :] = jnp.concatenate([low, tail, blank], axis=1)

    pick = pick_rows(
        info[6], labels_main.at[group], labels_rest.at[group], states, main, rest, put
    )
    lax.fori_loop(0, out.shape[0] // LANES, pick, 0, unroll=True)


def cross_kernel(
    info, labels_main, labels_rest, ids, rows, states, near, out, picked, main, rest
):
    size = rows.shape[0]
    group = 1 - info[5]
    base = info[6]

    def put(at, low, tail):
        blank = jnp.zeros((LANES, LANES - MAIN - LONGEST), F32)
        here = jnp.concatenate([low, tail, blank], axis=1)
        picked[pl.ds(at, LANES), :] = near[pl.ds(at, LANES), :] + here

    pick = pick_rows(base, labels_main.at[group], labels_rest.at[group], states, main, rest, put)
    lax.fori_loop(0, near.shape[0] // LANES, pick, 0, unroll=True)
    keys = picked[...].astype(BF)[:, 0:size]
    turned = picked[...].T.astype(BF)
    wanted = base + lax.broadcasted_iota(jnp.int32, (near.shape[0], LANES), 0)
    allowed = wanted >= 0

    for i in range(rows.shape[1] // LANES):
        at = slice(i * LANES, (i + 1) * LANES)
        mine = rows[:, at]
        far = ids[:, at] - wanted
        close = (far >= 0) & (far < WINDOW) & allowed
        scores = matmul(keys, mine) * (1.0 / math.sqrt(size))
        scores = jnp.where(close, scores, FLOOR_SCORE)
        weights = jnp.exp(scores - jnp.max(scores, axis=0, keepdims=True))
        total = jnp.sum(weights, axis=0, keepdims=True)
        reached = matmul(turned, weights.astype(BF))[0:size] / total
        out[:, at] = (mine.astype(F32) + reached).astype(BF)


def shift(x, axis, by):
    n = lax.axis_size(axis)
    return lax.ppermute(x, axis, [(i, (i + by) % n) for i in range(n)])


def over_plane(copies):
    near = lax.all_to_all(copies, PLANE, 0, 0, tiled=True)
    return near, shift(near, "c", 1)


def over_z(four):
    half = four.shape[0] // 2
    after = shift(four, Z, 1)
    before = shift(four, Z, -1)
    return [four, after, before, shift(four[:half], Z, 2), shift(four[half:], Z, -2)]


def layer(byte_states, patch_ids, slot_patch, pool_gain, w_in, attn_gain, w_qkv, w_out, w_down):
    n_z = lax.axis_size(Z)
    n_zl = lax.axis_size(ZL)
    n_yl = lax.axis_size("yl")
    n_head = lax.axis_size(HEAD)
    patches = slot_patch.shape[0]
    rows_z = patches // n_z
    rows_each = rows_z // n_yl
    bytes_here, cross_size = byte_states.shape
    info = jnp.stack(
        [
            lax.axis_index("c"),
            lax.axis_index("yl"),
            lax.axis_index(("yh", "x")),
            lax.axis_index(ZL),
            lax.axis_index(Z),
            lax.axis_index("zp"),
            patch_ids[0] - (WINDOW - 1),
        ]
    ).astype(jnp.int32)
    n_plane = lax.axis_size(PLANE)
    slots = slot_patch[:, None]
    rows = byte_states.T
    first = info[1] == 0

    w_in_parts = w_in.reshape(w_in.shape[0], n_yl, -1).transpose(1, 0, 2)
    w_in_parts = jnp.broadcast_to(w_in_parts[None], (n_z, *w_in_parts.shape))
    w_in_parts = w_in_parts.reshape(n_z * n_yl, w_in.shape[0], -1)
    w_in_here = lax.all_to_all(w_in_parts, SEQ, 0, 0, tiled=True)
    w_in_here = w_in_here.reshape(-1, w_in_parts.shape[2])

    halves = [
        jnp.concatenate([w_qkv[:, j, k * HEAD_SIZE : (k + 1) * HEAD_SIZE] for j in range(3)], axis=1)
        for k in range(n_yl)
    ]
    depth = w_qkv.shape[0]
    down_pieces = [w_down[:depth], w_down[depth:]]
    sent = jnp.concatenate([jnp.where(first, halves[1], halves[0]), *down_pieces], axis=1)
    came = shift(sent, "yl", 1)
    kept = jnp.concatenate([jnp.where(first, halves[0], halves[1]), *down_pieces], axis=1)
    low = jnp.where(first, kept, came)
    high = jnp.where(first, came, kept)
    wide = halves[0].shape[1]
    part = w_down.shape[1]
    down_both = [
        jnp.concatenate([v[:, wide : wide + part], v[:, wide + part :]], axis=0) for v in (low, high)
    ]
    blank = jnp.zeros((2 * depth, LANES - 2 * part), BF)
    mine = jnp.concatenate([low[:, :wide], high[:, :wide]], axis=0)
    weights = lax.all_gather(
        jnp.concatenate([mine, *down_both, blank], axis=1), Z, axis=0, tiled=True
    )

    packed = jax.ShapeDtypeStruct((n_z, rows_each // 2 + LONGEST, LANES), BF)
    pool_inputs = [info, slots, patch_ids[None, :], rows]
    sent = local_call(functools.partial(pool_kernel, True), packed, pool_inputs, scalars=1)
    came = shift(sent, "yl", 1)
    kept = local_call(functools.partial(pool_kernel, False), packed, pool_inputs, scalars=1)
    pooled = (kept.astype(F32) + came.astype(F32)).astype(BF)
    pooled = lax.all_to_all(pooled, Z, 0, 0, tiled=True)
    pooled = local_call(
        sum_kernel, jax.ShapeDtypeStruct((n_plane, *pooled.shape[1:]), BF), [pooled]
    )
    embed = local_call(
        embed_kernel,
        jax.ShapeDtypeStruct((n_plane, rows_z, w_in_here.shape[1]), BF),
        [info, *over_plane(pooled), pool_gain.reshape(n_head, cross_size), w_in_here],
        scratch=[pltpu.VMEM((n_head, rows_z, cross_size), F32)],
        scalars=1,
    )
    own_embed, other_embed = over_plane(embed)
    queries, kv, down_here = local_call(
        project_kernel,
        [
            jax.ShapeDtypeStruct((rows_z, HEAD_SIZE), BF),
            jax.ShapeDtypeStruct((n_z // n_zl, rows_z, 2 * HEAD_SIZE), BF),
            jax.ShapeDtypeStruct((weights.shape[0], LANES), BF),
        ],
        [info, own_embed, other_embed, attn_gain.reshape(n_head, -1), weights],
        scalars=1,
    )
    labels = slot_patch.reshape(n_z // n_zl, n_zl, rows_z).transpose(1, 0, 2).reshape(n_zl, -1)
    kv = lax.all_to_all(kv, "zh", 0, 0, tiled=True).reshape(-1, kv.shape[2])
    kept, sent = local_call(
        attend_kernel,
        [jax.ShapeDtypeStruct((rows_each, HEAD_SIZE), BF)] * 2,
        [
            info,
            queries,
            slots,
            labels,
            *over_z(kv),
        ],
        scratch=[pltpu.VMEM((rows_z, patches), F32), pltpu.VMEM((rows_z, HEAD_SIZE), F32)],
        scalars=1,
    )
    out_part = local_call(
        out_kernel,
        jax.ShapeDtypeStruct((n_head, rows_each, w_out.shape[1] // n_head), BF),
        [info, kept, shift(sent, "yl", 1), w_out],
        scalars=1,
    )
    arrived = lax.all_to_all(out_part, HEAD, 0, 0, tiled=True)
    stream, down_part = local_call(
        down_kernel,
        [
            jax.ShapeDtypeStruct((rows_each, w_in.shape[1]), BF),
            jax.ShapeDtypeStruct((n_head, rows_each // 2 + LONGEST, LANES), BF),
        ],
        [info, arrived, own_embed, down_here],
        scalars=1,
    )
    states = lax.all_to_all(down_part, HEAD, 0, 0, tiled=True)
    n_skip = lax.axis_size(SKIP)
    states = local_call(
        sum_kernel, jax.ShapeDtypeStruct((n_skip, *states.shape[1:]), BF), [states]
    )
    states = lax.all_to_all(states, SKIP, 0, 0, tiled=True)
    others = shift(states, "zp", 1)
    by_source = slot_patch.reshape(-1, 2, n_yl, rows_each).transpose(1, 0, 2, 3)
    by_source = by_source.reshape(2, n_skip, rows_each)
    labels_main = by_source.reshape(2, n_skip, 2, -1).transpose(0, 2, 1, 3).reshape(2, 2, -1)
    labels_rest = by_source.reshape(2, n_skip, -1, LONGEST).transpose(0, 2, 1, 3)
    labels_rest = labels_rest.reshape(2, rows_each // LONGEST, -1)
    capacity = bytes_here + LANES
    room = [
        pltpu.VMEM((n_skip * rows_each // 2, LANES), BF),
        pltpu.VMEM((n_skip * LONGEST, LANES), BF),
    ]
    near = local_call(
        near_kernel,
        jax.ShapeDtypeStruct((capacity, LANES), F32),
        [info, labels_main, labels_rest, states],
        scratch=room,
        scalars=1,
    )
    byte_out = local_call(
        cross_kernel,
        jax.ShapeDtypeStruct((cross_size, bytes_here), BF),
        [info, labels_main, labels_rest, patch_ids[None, :], rows, others, near],
        scratch=[pltpu.VMEM((capacity, LANES), F32), *room],
        scalars=1,
    ).T
    return (stream, byte_out)


def solution(mesh):
    torus = Mesh(
        mesh.devices.reshape(4, 2, 2, 2, 2, 4, 2), ("zh", "zm", "zp", "yl", "yh", "x", "c")
    )
    return jax.shard_map(
        layer,
        mesh=torus,
        in_specs=(
            P(SEQ, HEAD),
            P(SEQ),
            P(),
            P(),
            P(SEQ, HEAD),
            P(),
            P(SEQ, None, HEAD),
            P(HEAD, None),
            P(HEAD, SEQ),
        ),
        out_specs=(P(SEQ, HEAD), P(SEQ, HEAD)),
        check_vma=False,
    )
```

```python
import functools
import math

import jax
import jax.numpy as jnp
from jax import lax
from jax.experimental import pallas as pl
from jax.experimental.pallas import tpu as pltpu
from jax.sharding import Mesh
from jax.sharding import PartitionSpec as P


HEAD_SIZE = 128
WINDOW = 8
LONGEST = 16
ZL = ("zm", "zp")
Z = ("zh", "zm", "zp")
SEQ = ("zh", "zm", "zp", "yl")
SKIP = ("zh", "zm", "yl")
PLANE = ("yl", "yh", "x")
HEAD = ("yh", "x", "c")
EPSILON = 1e-05
FLOOR_SCORE = -1e30
BF = jnp.bfloat16
F32 = jnp.float32
MAIN = 64
LANES = 128


VMEM = pl.BlockSpec(memory_space=pltpu.VMEM)
SMEM = pl.BlockSpec(memory_space=pltpu.SMEM)


def local_call(kernel, out, inputs, scratch=(), scalars=0, left=0, flops=10**8, moved=10**6):
    specs = [SMEM] * scalars + [VMEM] * (len(inputs) - scalars - left)
    specs = specs + [pl.BlockSpec(memory_space=pl.ANY)] * left
    many = isinstance(out, (list, tuple))
    return pl.pallas_call(
        kernel,
        out_shape=out,
        in_specs=specs,
        out_specs=[VMEM] * len(out) if many else VMEM,
        scratch_shapes=list(scratch),
        compiler_params=pltpu.CompilerParams(vmem_limit_bytes=48 << 20),
        cost_estimate=pl.CostEstimate(flops=flops, bytes_accessed=moved, transcendentals=0),
    )(*inputs)


def matmul(a, b):
    return lax.dot_general(a, b, (((1,), (0,)), ((), ())), preferred_element_type=F32)


def matmul_t(a, b):
    return lax.dot_general(a, b, (((1,), (1,)), ((), ())), preferred_element_type=F32)


def pool_kernel(flip, info, slots, ids, rows, out):
    blocks, packed_rows, _ = out.shape
    count = slots.shape[0] // (2 * blocks)
    half = count // 2
    group = packed_rows - half
    blank = jnp.zeros((group, LANES - group * (count // group)), F32)
    side = 1 - info[1] if flip else info[1]

    def step(i, unused):
        at = pl.multiple_of((2 * i + side) * count, count)
        match = jnp.where(slots[pl.ds(at, count), :] == ids[...], 1.0, 0.0).astype(BF)
        part = matmul_t(match, rows[...])
        out[i, 0:half, 0:MAIN] = part[0:half, 0:MAIN].astype(BF)
        out[i, 0:half, MAIN:LANES] = part[half:count, 0:MAIN].astype(BF)
        rest = [part[group * g : group * (g + 1), MAIN:] for g in range(count // group)]
        out[i, half:packed_rows, :] = jnp.concatenate(rest + [blank], axis=1).astype(BF)
        return unused

    lax.fori_loop(0, blocks, step, 0, unroll=4)


def sum_kernel(arrived, out):
    total = jnp.zeros(arrived.shape[1:], F32)
    for i in range(arrived.shape[0]):
        total = total + arrived[i].astype(F32)
    held = total.astype(BF)
    for i in range(out.shape[0]):
        out[i] = held


def embed_kernel(pooled, gain, w_in, out, keep):
    heads, count, size = keep.shape
    each = count // 2
    half = each // 2
    spare = size - MAIN
    group = pooled.shape[1] - half
    square = jnp.zeros((count, 1), F32)
    for h in range(heads):
        two = [pooled[y * heads + h].astype(F32) for y in range(2)]
        main = [v[0:half, at : at + MAIN] for v in two for at in (0, MAIN)]
        main = jnp.concatenate(main, axis=0)
        rest = [v[half:, spare * g : spare * (g + 1)] for v in two for g in range(each // group)]
        rest = jnp.concatenate(rest, axis=0)
        keep[h, :, 0:MAIN] = main
        keep[h, :, MAIN:size] = rest
        square = square + jnp.sum(main * main, axis=1, keepdims=True)
        square = square + jnp.sum(rest * rest, axis=1, keepdims=True)
    scale = lax.rsqrt(square / (heads * size) + EPSILON)
    total = jnp.zeros(out.shape[1:], F32)
    for h in range(heads):
        normed = keep[h] * scale * gain[h : h + 1, :]
        total = total + matmul(normed.astype(BF), w_in[h * size : (h + 1) * size, :])
    held = total.astype(BF)
    for i in range(out.shape[0]):
        out[i] = held


def project_kernel(info, own, other, gain, weights, queries, kv, down, held, arrived):
    planes = own.shape[0] // 2
    count, width = own.shape[1:]
    size = 2 * width
    columns = 3 * HEAD_SIZE

    def copy(h):
        at = slice(h * size, (h + 1) * size)
        return pltpu.make_async_copy(weights.at[at, :], held.at[at, :], arrived.at[h])

    for h in range(2 * planes):
        copy(h).start()
    square = jnp.zeros((count, width), F32)
    for source in (own, other):
        for b in range(2 * planes):
            wide = source[b].astype(F32)
            square = square + wide * wide
    square = jnp.sum(square, axis=1, keepdims=True)
    scale = lax.rsqrt(square / (2 * planes * size) + EPSILON)
    total = jnp.zeros((count, columns), F32)
    for p in range(planes):
        copy(2 * p).wait()
        copy(2 * p + 1).wait()
        for side, source in ((0, own), (1, other)):
            core = info[0] if side == 0 else 1 - info[0]
            h = 2 * p + core
            both = jnp.concatenate([source[p], source[planes + p]], axis=1).astype(F32)
            attn_in = both * scale * gain[pl.ds(h, 1), :]
            at = pl.multiple_of(h * size, size)
            total = total + matmul(attn_in.astype(BF), held[pl.ds(at, size), 0:columns])
    queries[...] = total[:, 0:HEAD_SIZE].astype(BF)
    both = total[:, HEAD_SIZE:].astype(BF)
    for i in range(kv.shape[0]):
        kv[i] = both
    down[...] = held[:, columns:]


def attend_kernel(info, queries, slots, labels, *rest):
    pieces, keep, send, scores, held = rest[:-4], rest[-4], rest[-3], rest[-2], rest[-1]
    query = queries[...]
    own = pl.multiple_of(info[4] * query.shape[0], query.shape[0])
    mine = slots[pl.ds(own, query.shape[0]), :]
    peak = jnp.full((query.shape[0], 1), FLOOR_SCORE, F32)
    turns = ((0, 0), (3, 0), (1, 0), (2, 0), (2, labels.shape[1] // 2))
    start = 0
    for piece, (turn, at) in zip(pieces, turns):
        size = piece.shape[0]
        here = labels[pl.ds((info[3] + turn) % 4, 1), at : at + size]
        part = matmul_t(query, piece[:, 0:HEAD_SIZE]) * (1.0 / math.sqrt(HEAD_SIZE))
        part = jnp.where(here <= mine, part, FLOOR_SCORE)
        scores[:, start : start + size] = part
        peak = jnp.maximum(peak, jnp.max(part, axis=1, keepdims=True))
        start += size
    total = jnp.zeros_like(peak)
    mixed = jnp.zeros(query.shape, F32)
    start = 0
    for piece in pieces:
        size = piece.shape[0]
        weights = jnp.exp(scores[:, start : start + size] - peak)
        total = total + jnp.sum(weights, axis=1, keepdims=True)
        mixed = mixed + matmul(weights.astype(BF), piece[:, HEAD_SIZE:])
        start += size
    held[...] = mixed / total
    count = keep.shape[0]
    at = pl.multiple_of(info[1] * count, count)
    keep[...] = held[pl.ds(at, count), :].astype(BF)
    at = pl.multiple_of((1 - info[1]) * count, count)
    send[...] = held[pl.ds(at, count), :].astype(BF)


def out_kernel(info, kept, came, w_out, out):
    mine = kept[...]
    theirs = came[...]
    width = out.shape[2]
    at = pl.multiple_of(info[1] * HEAD_SIZE, HEAD_SIZE)
    other = pl.multiple_of((1 - info[1]) * HEAD_SIZE, HEAD_SIZE)
    for h in range(out.shape[0]):
        cols = slice(h * width, (h + 1) * width)
        part = matmul(mine, w_out[pl.ds(at, HEAD_SIZE), cols])
        part = part + matmul(theirs, w_out[pl.ds(other, HEAD_SIZE), cols])
        out[h] = part.astype(BF)


def down_kernel(info, arrived, embed, w_down, stream, out):
    count, width = stream.shape
    half = count // 2
    planes = embed.shape[0] // 2
    size = MAIN + LONGEST
    at = pl.multiple_of(info[1] * count, count)
    low = embed[info[2], pl.ds(at, count), :]
    high = embed[planes + info[2], pl.ds(at, count), :]
    total = jnp.concatenate([low, high], axis=1).astype(F32)
    added = jnp.zeros(total.shape, F32)
    for h in range(arrived.shape[0]):
        added = added + arrived[h].astype(F32)
    held = (total + added).astype(BF)
    stream[...] = held
    group = out.shape[1] - half
    blank = jnp.zeros((group, LANES - LONGEST * (count // group)), F32)
    for h in range(out.shape[0]):
        part = matmul(held, w_down[h * width : (h + 1) * width, :])
        out[h, 0:half, 0:MAIN] = part[0:half, 0:MAIN].astype(BF)
        out[h, 0:half, MAIN:LANES] = part[half:, 0:MAIN].astype(BF)
        rest = [part[group * g : group * (g + 1), MAIN:size] for g in range(count // group)]
        out[h, half:, :] = jnp.concatenate(rest + [blank], axis=1).astype(BF)


def pick_rows(base, labels_main, labels_rest, states, main, rest, put):
    groups = labels_rest.shape[0]
    half = groups * LONGEST // 2
    for i in range(states.shape[0]):
        main[i * half : (i + 1) * half, :] = states[i, 0:half, :]
        rest[i * LONGEST : (i + 1) * LONGEST, :] = states[i, half:, :]
    step = LANES

    def hot(at, label):
        wanted = base + at + lax.broadcasted_iota(jnp.int32, (step, label.shape[1]), 0)
        return jnp.where(wanted == label, 1.0, 0.0).astype(BF)

    def pick(i, unused):
        at = pl.multiple_of(i * step, step)
        low = matmul(hot(at, labels_main[0:1, :]), main[...])
        high = matmul(hot(at, labels_main[1:2, :]), main[...])
        tail = jnp.zeros((step, LONGEST), F32)
        for g in range(groups):
            here = matmul(hot(at, labels_rest[g : g + 1, :]), rest[...])
            tail = tail + here[:, g * LONGEST : (g + 1) * LONGEST]
        put(at, low[:, 0:MAIN] + high[:, MAIN:LANES], tail)
        return unused

    return pick


def near_kernel(info, labels_main, labels_rest, states, out, main, rest):
    group = info[5]

    def put(at, low, tail):
        blank = jnp.zeros((LANES, LANES - MAIN - LONGEST), F32)
        out[pl.ds(at, LANES), :] = jnp.concatenate([low, tail, blank], axis=1)

    pick = pick_rows(
        info[6], labels_main.at[group], labels_rest.at[group], states, main, rest, put
    )
    lax.fori_loop(0, out.shape[0] // LANES, pick, 0, unroll=True)


def cross_kernel(
    info, labels_main, labels_rest, ids, rows, states, near, out, picked, main, rest
):
    size = rows.shape[0]
    group = 1 - info[5]
    base = info[6]

    def put(at, low, tail):
        blank = jnp.zeros((LANES, LANES - MAIN - LONGEST), F32)
        here = jnp.concatenate([low, tail, blank], axis=1)
        picked[pl.ds(at, LANES), :] = near[pl.ds(at, LANES), :] + here

    pick = pick_rows(base, labels_main.at[group], labels_rest.at[group], states, main, rest, put)
    lax.fori_loop(0, near.shape[0] // LANES, pick, 0, unroll=True)
    keys = picked[...].astype(BF)[:, 0:size]
    turned = picked[...].T.astype(BF)
    wanted = base + lax.broadcasted_iota(jnp.int32, (near.shape[0], LANES), 0)
    allowed = wanted >= 0

    for i in range(rows.shape[1] // LANES):
        at = slice(i * LANES, (i + 1) * LANES)
        mine = rows[:, at]
        far = ids[:, at] - wanted
        close = (far >= 0) & (far < WINDOW) & allowed
        scores = matmul(keys, mine) * (1.0 / math.sqrt(size))
        scores = jnp.where(close, scores, FLOOR_SCORE)
        weights = jnp.exp(scores - jnp.max(scores, axis=0, keepdims=True))
        total = jnp.sum(weights, axis=0, keepdims=True)
        reached = matmul(turned, weights.astype(BF))[0:size] / total
        out[:, at] = (mine.astype(F32) + reached).astype(BF)


def shift(x, axis, by):
    n = lax.axis_size(axis)
    return lax.ppermute(x, axis, [(i, (i + by) % n) for i in range(n)])


def over_plane(copies):
    near = lax.all_to_all(copies, PLANE, 0, 0, tiled=True)
    return near, shift(near, "c", 1)


def over_z(four):
    half = four.shape[0] // 2
    after = shift(four, Z, 1)
    before = shift(four, Z, -1)
    return [four, after, before, shift(four[:half], Z, 2), shift(four[half:], Z, -2)]


def layer(byte_states, patch_ids, slot_patch, pool_gain, w_in, attn_gain, w_qkv, w_out, w_down):
    n_z = lax.axis_size(Z)
    n_zl = lax.axis_size(ZL)
    n_yl = lax.axis_size("yl")
    n_head = lax.axis_size(HEAD)
    patches = slot_patch.shape[0]
    rows_z = patches // n_z
    rows_each = rows_z // n_yl
    bytes_here, cross_size = byte_states.shape
    info = jnp.stack(
        [
            lax.axis_index("c"),
            lax.axis_index("yl"),
            lax.axis_index(("yh", "x")),
            lax.axis_index(ZL),
            lax.axis_index(Z),
            lax.axis_index("zp"),
            patch_ids[0] - (WINDOW - 1),
        ]
    ).astype(jnp.int32)
    n_plane = lax.axis_size(PLANE)
    slots = slot_patch[:, None]
    rows = byte_states.T
    first = info[1] == 0

    halves = [
        jnp.concatenate([w_qkv[:, j, k * HEAD_SIZE : (k + 1) * HEAD_SIZE] for j in range(3)], axis=1)
        for k in range(n_yl)
    ]
    depth = w_qkv.shape[0]
    down_pieces = [w_down[:depth], w_down[depth:]]
    in_width = w_in.shape[1] // n_yl
    in_halves = [w_in[:, k * in_width : (k + 1) * in_width] for k in range(n_yl)]

    def payload(top, bottom):
        top = jnp.concatenate([top, *down_pieces], axis=1)
        fill = jnp.zeros((bottom.shape[0], top.shape[1] - in_width), BF)
        return jnp.concatenate([top, jnp.concatenate([bottom, fill], axis=1)], axis=0)

    swapped = [jnp.where(first, v[1], v[0]) for v in (halves, in_halves)]
    stayed = [jnp.where(first, v[0], v[1]) for v in (halves, in_halves)]
    came = shift(payload(*swapped), "yl", 1)
    w_in_came = came[depth:, :in_width]
    w_in_both = [jnp.where(first, stayed[1], w_in_came), jnp.where(first, w_in_came, stayed[1])]
    w_in_both = jnp.concatenate(w_in_both, axis=0)
    w_in_here = lax.all_to_all(
        jnp.broadcast_to(w_in_both[None], (n_z, *w_in_both.shape)), Z, 0, 0, tiled=True
    )
    w_in_here = w_in_here.reshape(-1, in_width)
    kept = jnp.concatenate([stayed[0], *down_pieces], axis=1)
    came = came[:depth]
    low = jnp.where(first, kept, came)
    high = jnp.where(first, came, kept)
    wide = halves[0].shape[1]
    part = w_down.shape[1]
    down_both = [
        jnp.concatenate([v[:, wide : wide + part], v[:, wide + part :]], axis=0) for v in (low, high)
    ]
    blank = jnp.zeros((2 * depth, LANES - 2 * part), BF)
    mine = jnp.concatenate([low[:, :wide], high[:, :wide]], axis=0)
    weights = lax.all_gather(
        jnp.concatenate([mine, *down_both, blank], axis=1), Z, axis=0, tiled=True
    )

    packed = jax.ShapeDtypeStruct((n_z, rows_each // 2 + LONGEST, LANES), BF)
    pool_inputs = [info, slots, patch_ids[None, :], rows]
    sent = local_call(functools.partial(pool_kernel, True), packed, pool_inputs, scalars=1)
    came = shift(sent, "yl", 1)
    kept = local_call(functools.partial(pool_kernel, False), packed, pool_inputs, scalars=1)
    pooled = (kept.astype(F32) + came.astype(F32)).astype(BF)
    pooled = lax.all_to_all(pooled, Z, 0, 0, tiled=True)
    pooled = local_call(
        sum_kernel, jax.ShapeDtypeStruct((2 * n_plane, *pooled.shape[1:]), BF), [pooled]
    )
    pooled = lax.all_to_all(pooled, (*PLANE, "c"), 0, 0, tiled=True)
    embed = local_call(
        embed_kernel,
        jax.ShapeDtypeStruct((n_plane, rows_z, w_in_here.shape[1]), BF),
        [pooled, pool_gain.reshape(n_head, cross_size), w_in_here],
        scratch=[pltpu.VMEM((n_head, rows_z, cross_size), F32)],
    )
    own_embed, other_embed = over_plane(embed)
    queries, kv, down_here = local_call(
        project_kernel,
        [
            jax.ShapeDtypeStruct((rows_z, HEAD_SIZE), BF),
            jax.ShapeDtypeStruct((n_z // n_zl, rows_z, 2 * HEAD_SIZE), BF),
            jax.ShapeDtypeStruct((weights.shape[0], LANES), BF),
        ],
        [info, own_embed, other_embed, attn_gain.reshape(n_head, -1), weights],
        scratch=[pltpu.VMEM(weights.shape, BF), pltpu.SemaphoreType.DMA((n_head,))],
        scalars=1,
        left=1,
    )
    labels = slot_patch.reshape(n_z // n_zl, n_zl, rows_z).transpose(1, 0, 2).reshape(n_zl, -1)
    kv = lax.all_to_all(kv, "zh", 0, 0, tiled=True).reshape(-1, kv.shape[2])
    kept, sent = local_call(
        attend_kernel,
        [jax.ShapeDtypeStruct((rows_each, HEAD_SIZE), BF)] * 2,
        [
            info,
            queries,
            slots,
            labels,
            *over_z(kv),
        ],
        scratch=[pltpu.VMEM((rows_z, patches), F32), pltpu.VMEM((rows_z, HEAD_SIZE), F32)],
        scalars=1,
    )
    out_part = local_call(
        out_kernel,
        jax.ShapeDtypeStruct((n_head, rows_each, w_out.shape[1] // n_head), BF),
        [info, kept, shift(sent, "yl", 1), w_out],
        scalars=1,
    )
    arrived = lax.all_to_all(out_part, HEAD, 0, 0, tiled=True)
    stream, down_part = local_call(
        down_kernel,
        [
            jax.ShapeDtypeStruct((rows_each, w_in.shape[1]), BF),
            jax.ShapeDtypeStruct((n_head, rows_each // 2 + LONGEST, LANES), BF),
        ],
        [info, arrived, own_embed, down_here],
        scalars=1,
    )
    states = lax.all_to_all(down_part, HEAD, 0, 0, tiled=True)
    n_skip = lax.axis_size(SKIP)
    states = local_call(
        sum_kernel, jax.ShapeDtypeStruct((n_skip, *states.shape[1:]), BF), [states]
    )
    states = lax.all_to_all(states, SKIP, 0, 0, tiled=True)
    others = shift(states, "zp", 1)
    by_source = slot_patch.reshape(-1, 2, n_yl, rows_each).transpose(1, 0, 2, 3)
    by_source = by_source.reshape(2, n_skip, rows_each)
    labels_main = by_source.reshape(2, n_skip, 2, -1).transpose(0, 2, 1, 3).reshape(2, 2, -1)
    labels_rest = by_source.reshape(2, n_skip, -1, LONGEST).transpose(0, 2, 1, 3)
    labels_rest = labels_rest.reshape(2, rows_each // LONGEST, -1)
    capacity = bytes_here + LANES
    room = [
        pltpu.VMEM((n_skip * rows_each // 2, LANES), BF),
        pltpu.VMEM((n_skip * LONGEST, LANES), BF),
    ]
    near = local_call(
        near_kernel,
        jax.ShapeDtypeStruct((capacity, LANES), F32),
        [info, labels_main, labels_rest, states],
        scratch=room,
        scalars=1,
    )
    byte_out = local_call(
        cross_kernel,
        jax.ShapeDtypeStruct((cross_size, bytes_here), BF),
        [info, labels_main, labels_rest, patch_ids[None, :], rows, others, near],
        scratch=[pltpu.VMEM((capacity, LANES), F32), *room],
        scalars=1,
    ).T
    return (stream, byte_out)


def solution(mesh):
    torus = Mesh(
        mesh.devices.reshape(4, 2, 2, 2, 2, 4, 2), ("zh", "zm", "zp", "yl", "yh", "x", "c")
    )
    return jax.shard_map(
        layer,
        mesh=torus,
        in_specs=(
            P(SEQ, HEAD),
            P(SEQ),
            P(),
            P(),
            P(SEQ, HEAD),
            P(),
            P(SEQ, None, HEAD),
            P(HEAD, None),
            P(HEAD, SEQ),
        ),
        out_specs=(P(SEQ, HEAD), P(SEQ, HEAD)),
        check_vma=False,
    )
```

```python
import functools
import math

import jax
import jax.numpy as jnp
from jax import lax
from jax.experimental import pallas as pl
from jax.experimental.pallas import tpu as pltpu
from jax.sharding import Mesh
from jax.sharding import PartitionSpec as P


HEAD_SIZE = 128
WINDOW = 8
LONGEST = 16
ZL = ("zm", "zp")
Z = ("zh", "zm", "zp")
SEQ = ("zh", "zm", "zp", "yl")
SKIP = ("zh", "zm", "yl")
PLANE = ("yl", "yh", "x")
HEAD = ("yh", "x", "c")
EPSILON = 1e-05
FLOOR_SCORE = -1e30
BF = jnp.bfloat16
F32 = jnp.float32
MAIN = 64
LANES = 128


VMEM = pl.BlockSpec(memory_space=pltpu.VMEM)
SMEM = pl.BlockSpec(memory_space=pltpu.SMEM)


def local_call(kernel, out, inputs, scratch=(), scalars=0, last=(), flops=10**8, moved=10**6):
    specs = [SMEM] * scalars + [VMEM] * (len(inputs) - scalars - len(last)) + list(last)
    many = isinstance(out, (list, tuple))
    return pl.pallas_call(
        kernel,
        out_shape=out,
        grid=(1,) if last else (),
        in_specs=specs,
        out_specs=[VMEM] * len(out) if many else VMEM,
        scratch_shapes=list(scratch),
        compiler_params=pltpu.CompilerParams(vmem_limit_bytes=48 << 20),
        cost_estimate=pl.CostEstimate(flops=flops, bytes_accessed=moved, transcendentals=0),
    )(*inputs)


def matmul(a, b):
    return lax.dot_general(a, b, (((1,), (0,)), ((), ())), preferred_element_type=F32)


def matmul_t(a, b):
    return lax.dot_general(a, b, (((1,), (1,)), ((), ())), preferred_element_type=F32)


def split_kernel(w_in, out):
    width = out.shape[2]
    for i in range(out.shape[0]):
        out[i] = w_in[:, (i % 2) * width : (i % 2 + 1) * width]


def take_kernel(weights, out):
    out[...] = weights[...]


def pool_kernel(flip, info, slots, ids, rows, out):
    blocks, packed_rows, _ = out.shape
    count = slots.shape[0] // (2 * blocks)
    half = count // 2
    group = packed_rows - half
    blank = jnp.zeros((group, LANES - group * (count // group)), F32)
    side = 1 - info[1] if flip else info[1]

    def step(i, unused):
        at = pl.multiple_of((2 * i + side) * count, count)
        match = jnp.where(slots[pl.ds(at, count), :] == ids[...], 1.0, 0.0).astype(BF)
        part = matmul_t(match, rows[...])
        out[i, 0:half, 0:MAIN] = part[0:half, 0:MAIN].astype(BF)
        out[i, 0:half, MAIN:LANES] = part[half:count, 0:MAIN].astype(BF)
        rest = [part[group * g : group * (g + 1), MAIN:] for g in range(count // group)]
        out[i, half:packed_rows, :] = jnp.concatenate(rest + [blank], axis=1).astype(BF)
        return unused

    lax.fori_loop(0, blocks, step, 0, unroll=4)


def sum_kernel(arrived, out):
    total = jnp.zeros(arrived.shape[1:], F32)
    for i in range(arrived.shape[0]):
        total = total + arrived[i].astype(F32)
    held = total.astype(BF)
    for i in range(out.shape[0]):
        out[i] = held


def embed_kernel(pooled, gain, w_in, out, keep):
    heads, count, size = keep.shape
    each = count // 2
    half = each // 2
    spare = size - MAIN
    group = pooled.shape[1] - half
    square = jnp.zeros((count, 1), F32)
    for h in range(heads):
        two = [pooled[y * heads + h].astype(F32) for y in range(2)]
        main = [v[0:half, at : at + MAIN] for v in two for at in (0, MAIN)]
        main = jnp.concatenate(main, axis=0)
        rest = [v[half:, spare * g : spare * (g + 1)] for v in two for g in range(each // group)]
        rest = jnp.concatenate(rest, axis=0)
        keep[h, :, 0:MAIN] = main
        keep[h, :, MAIN:size] = rest
        square = square + jnp.sum(main * main, axis=1, keepdims=True)
        square = square + jnp.sum(rest * rest, axis=1, keepdims=True)
    scale = lax.rsqrt(square / (heads * size) + EPSILON)
    total = jnp.zeros(out.shape[1:], F32)
    for h in range(heads):
        normed = keep[h] * scale * gain[h : h + 1, :]
        total = total + matmul(normed.astype(BF), w_in[h * size : (h + 1) * size, :])
    held = total.astype(BF)
    for i in range(out.shape[0]):
        out[i] = held


def project_kernel(info, own, other, gain, weights, queries, kv):
    planes = own.shape[0] // 2
    count, width = own.shape[1:]
    size = 2 * width
    columns = 3 * HEAD_SIZE
    square = jnp.zeros((count, width), F32)
    for source in (own, other):
        for b in range(2 * planes):
            wide = source[b].astype(F32)
            square = square + wide * wide
    square = jnp.sum(square, axis=1, keepdims=True)
    scale = lax.rsqrt(square / (2 * planes * size) + EPSILON)
    total = jnp.zeros((count, columns), F32)
    for side, source in ((0, own), (1, other)):
        core = info[0] if side == 0 else 1 - info[0]
        for p in range(planes):
            h = 2 * p + core
            both = jnp.concatenate([source[p], source[planes + p]], axis=1).astype(F32)
            attn_in = both * scale * gain[pl.ds(h, 1), :]
            at = pl.multiple_of(h * size, size)
            total = total + matmul(attn_in.astype(BF), weights[pl.ds(at, size), :])
    queries[...] = total[:, 0:HEAD_SIZE].astype(BF)
    held = total[:, HEAD_SIZE:].astype(BF)
    for i in range(kv.shape[0]):
        kv[i] = held


def attend_kernel(info, queries, slots, labels, *rest):
    pieces, out, scores = rest[:-2], rest[-2], rest[-1]
    query = queries[...]
    own = pl.multiple_of(info[4] * query.shape[0], query.shape[0])
    mine = slots[pl.ds(own, query.shape[0]), :]
    peak = jnp.full((query.shape[0], 1), FLOOR_SCORE, F32)
    turns = ((0, 0), (3, 0), (1, 0), (2, 0), (2, labels.shape[1] // 2))
    start = 0
    for piece, (turn, at) in zip(pieces, turns):
        size = piece.shape[0]
        here = labels[pl.ds((info[3] + turn) % 4, 1), at : at + size]
        part = matmul_t(query, piece[:, 0:HEAD_SIZE]) * (1.0 / math.sqrt(HEAD_SIZE))
        part = jnp.where(here <= mine, part, FLOOR_SCORE)
        scores[:, start : start + size] = part
        peak = jnp.maximum(peak, jnp.max(part, axis=1, keepdims=True))
        start += size
    total = jnp.zeros_like(peak)
    mixed = jnp.zeros(query.shape, F32)
    start = 0
    for piece in pieces:
        size = piece.shape[0]
        weights = jnp.exp(scores[:, start : start + size] - peak)
        total = total + jnp.sum(weights, axis=1, keepdims=True)
        mixed = mixed + matmul(weights.astype(BF), piece[:, HEAD_SIZE:])
        start += size
    out[...] = (mixed / total).astype(BF)


def out_kernel(flip, info, attended, w_out, out):
    count, width = out.shape[1:]
    planes = out.shape[0] // 2
    mine = attended[...]
    at = pl.multiple_of(info[1] * HEAD_SIZE, HEAD_SIZE)
    core = 1 - info[0] if flip else info[0]
    for p in range(planes):
        cols = pl.multiple_of((2 * p + core) * width, width)
        part = matmul(mine, w_out[pl.ds(at, HEAD_SIZE), pl.ds(cols, width)]).astype(BF)
        out[p] = part[0:count]
        out[planes + p] = part[count:]


def down_kernel(info, arrived, embed, w_down, stream, out):
    count, width = stream.shape
    half = count // 2
    planes = embed.shape[0] // 2
    size = MAIN + LONGEST
    at = pl.multiple_of(info[1] * count, count)
    low = embed[info[2], pl.ds(at, count), :]
    high = embed[planes + info[2], pl.ds(at, count), :]
    total = jnp.concatenate([low, high], axis=1).astype(F32)
    added = jnp.zeros(total.shape, F32)
    for h in range(arrived.shape[0]):
        added = added + arrived[h].astype(F32)
    held = (total + added).astype(BF)
    stream[...] = held
    group = out.shape[1] - half
    blank = jnp.zeros((group, LANES - LONGEST * (count // group)), F32)
    for h in range(out.shape[0]):
        part = matmul(held, w_down[h * width : (h + 1) * width, :])
        out[h, 0:half, 0:MAIN] = part[0:half, 0:MAIN].astype(BF)
        out[h, 0:half, MAIN:LANES] = part[half:, 0:MAIN].astype(BF)
        rest = [part[group * g : group * (g + 1), MAIN:size] for g in range(count // group)]
        out[h, half:, :] = jnp.concatenate(rest + [blank], axis=1).astype(BF)


def pick_rows(base, labels_main, labels_rest, states, main, rest, put):
    groups = labels_rest.shape[0]
    half = groups * LONGEST // 2
    for i in range(states.shape[0]):
        main[i * half : (i + 1) * half, :] = states[i, 0:half, :]
        rest[i * LONGEST : (i + 1) * LONGEST, :] = states[i, half:, :]
    step = LANES

    def hot(at, label):
        wanted = base + at + lax.broadcasted_iota(jnp.int32, (step, label.shape[1]), 0)
        return jnp.where(wanted == label, 1.0, 0.0).astype(BF)

    def pick(i, unused):
        at = pl.multiple_of(i * step, step)
        low = matmul(hot(at, labels_main[0:1, :]), main[...])
        high = matmul(hot(at, labels_main[1:2, :]), main[...])
        tail = jnp.zeros((step, LONGEST), F32)
        for g in range(groups):
            here = matmul(hot(at, labels_rest[g : g + 1, :]), rest[...])
            tail = tail + here[:, g * LONGEST : (g + 1) * LONGEST]
        put(at, low[:, 0:MAIN] + high[:, MAIN:LANES], tail)
        return unused

    return pick


def near_kernel(info, labels_main, labels_rest, states, out, main, rest):
    group = info[5]

    def put(at, low, tail):
        blank = jnp.zeros((LANES, LANES - MAIN - LONGEST), F32)
        out[pl.ds(at, LANES), :] = jnp.concatenate([low, tail, blank], axis=1)

    pick = pick_rows(
        info[6], labels_main.at[group], labels_rest.at[group], states, main, rest, put
    )
    lax.fori_loop(0, out.shape[0] // LANES, pick, 0, unroll=True)


def cross_kernel(
    info, labels_main, labels_rest, ids, rows, states, near, out, picked, main, rest
):
    size = rows.shape[0]
    group = 1 - info[5]
    base = info[6]

    def put(at, low, tail):
        blank = jnp.zeros((LANES, LANES - MAIN - LONGEST), F32)
        here = jnp.concatenate([low, tail, blank], axis=1)
        picked[pl.ds(at, LANES), :] = near[pl.ds(at, LANES), :] + here

    pick = pick_rows(base, labels_main.at[group], labels_rest.at[group], states, main, rest, put)
    lax.fori_loop(0, near.shape[0] // LANES, pick, 0, unroll=True)
    keys = picked[...].astype(BF)[:, 0:size]
    turned = picked[...].T.astype(BF)
    wanted = base + lax.broadcasted_iota(jnp.int32, (near.shape[0], LANES), 0)
    allowed = wanted >= 0

    for i in range(rows.shape[1] // LANES):
        at = slice(i * LANES, (i + 1) * LANES)
        mine = rows[:, at]
        far = ids[:, at] - wanted
        close = (far >= 0) & (far < WINDOW) & allowed
        scores = matmul(keys, mine) * (1.0 / math.sqrt(size))
        scores = jnp.where(close, scores, FLOOR_SCORE)
        weights = jnp.exp(scores - jnp.max(scores, axis=0, keepdims=True))
        total = jnp.sum(weights, axis=0, keepdims=True)
        reached = matmul(turned, weights.astype(BF))[0:size] / total
        out[:, at] = (mine.astype(F32) + reached).astype(BF)


def shift(x, axis, by):
    n = lax.axis_size(axis)
    return lax.ppermute(x, axis, [(i, (i + by) % n) for i in range(n)])


def over_plane(copies):
    near = lax.all_to_all(copies, PLANE, 0, 0, tiled=True)
    return near, shift(near, "c", 1)


def over_z(four):
    half = four.shape[0] // 2
    after = shift(four, Z, 1)
    before = shift(four, Z, -1)
    return [four, after, before, shift(four[:half], Z, 2), shift(four[half:], Z, -2)]


def layer(byte_states, patch_ids, slot_patch, pool_gain, w_in, attn_gain, w_qkv, w_out, w_down):
    n_z = lax.axis_size(Z)
    n_zl = lax.axis_size(ZL)
    n_yl = lax.axis_size("yl")
    n_head = lax.axis_size(HEAD)
    patches = slot_patch.shape[0]
    rows_z = patches // n_z
    rows_each = rows_z // n_yl
    bytes_here, cross_size = byte_states.shape
    info = jnp.stack(
        [
            lax.axis_index("c"),
            lax.axis_index("yl"),
            lax.axis_index(("yh", "x")),
            lax.axis_index(ZL),
            lax.axis_index(Z),
            lax.axis_index("zp"),
            patch_ids[0] - (WINDOW - 1),
        ]
    ).astype(jnp.int32)
    n_plane = lax.axis_size(PLANE)
    slots = slot_patch[:, None]
    rows = byte_states.T
    first = info[1] == 0

    w_in_parts = local_call(
        split_kernel,
        jax.ShapeDtypeStruct((n_z * n_yl, w_in.shape[0], w_in.shape[1] // n_yl), BF),
        [w_in],
    )
    w_in_here = lax.all_to_all(w_in_parts, SEQ, 0, 0, tiled=True)
    w_in_here = w_in_here.reshape(-1, w_in_parts.shape[2])

    halves = [
        jnp.concatenate([w_qkv[:, j, k * HEAD_SIZE : (k + 1) * HEAD_SIZE] for j in range(3)], axis=1)
        for k in range(n_yl)
    ]
    depth = w_qkv.shape[0]
    down_pieces = [w_down[:depth], w_down[depth:]]
    sent = jnp.concatenate([jnp.where(first, halves[1], halves[0]), *down_pieces], axis=1)
    came = shift(sent, "yl", 1)
    kept = jnp.concatenate([jnp.where(first, halves[0], halves[1]), *down_pieces], axis=1)
    low = jnp.where(first, kept, came)
    high = jnp.where(first, came, kept)
    wide = halves[0].shape[1]
    part = w_down.shape[1]
    down_both = [
        jnp.concatenate([v[:, wide : wide + part], v[:, wide + part :]], axis=0) for v in (low, high)
    ]
    blank = jnp.zeros((2 * depth, LANES - 2 * part), BF)
    mine = jnp.concatenate([low[:, :wide], high[:, :wide]], axis=0)
    weights = lax.all_gather(
        jnp.concatenate([mine, *down_both, blank], axis=1), Z, axis=0, tiled=True
    )

    packed = jax.ShapeDtypeStruct((n_z, rows_each // 2 + LONGEST, LANES), BF)
    pool_inputs = [info, slots, patch_ids[None, :], rows]
    sent = local_call(functools.partial(pool_kernel, True), packed, pool_inputs, scalars=1)
    came = shift(sent, "yl", 1)
    kept = local_call(functools.partial(pool_kernel, False), packed, pool_inputs, scalars=1)
    pooled = (kept.astype(F32) + came.astype(F32)).astype(BF)
    pooled = lax.all_to_all(pooled, Z, 0, 0, tiled=True)
    pooled = local_call(
        sum_kernel, jax.ShapeDtypeStruct((2 * n_plane, *pooled.shape[1:]), BF), [pooled]
    )
    pooled = lax.all_to_all(pooled, (*PLANE, "c"), 0, 0, tiled=True)
    embed = local_call(
        embed_kernel,
        jax.ShapeDtypeStruct((n_plane, rows_z, w_in_here.shape[1]), BF),
        [pooled, pool_gain.reshape(n_head, cross_size), w_in_here],
        scratch=[pltpu.VMEM((n_head, rows_z, cross_size), F32)],
    )
    own_embed, other_embed = over_plane(embed)
    queries, kv = local_call(
        project_kernel,
        [
            jax.ShapeDtypeStruct((rows_z, HEAD_SIZE), BF),
            jax.ShapeDtypeStruct((n_z // n_zl, rows_z, 2 * HEAD_SIZE), BF),
        ],
        [info, own_embed, other_embed, attn_gain.reshape(n_head, -1), weights],
        scalars=1,
        last=[pl.BlockSpec((weights.shape[0], wide), lambda i: (0, 0))],
    )
    down_here = local_call(
        take_kernel,
        jax.ShapeDtypeStruct((weights.shape[0], LANES), BF),
        [weights],
        last=[pl.BlockSpec((weights.shape[0], LANES), lambda i: (0, wide // LANES))],
    )
    labels = slot_patch.reshape(n_z // n_zl, n_zl, rows_z).transpose(1, 0, 2).reshape(n_zl, -1)
    kv = lax.all_to_all(kv, "zh", 0, 0, tiled=True).reshape(-1, kv.shape[2])
    attended = local_call(
        attend_kernel,
        jax.ShapeDtypeStruct((rows_z, HEAD_SIZE), BF),
        [info, queries, slots, labels, *over_z(kv)],
        scratch=[pltpu.VMEM((rows_z, patches), F32)],
        scalars=1,
    )
    out_shape = jax.ShapeDtypeStruct((n_plane, rows_each, w_out.shape[1] // n_head), BF)
    out_inputs = [info, attended, w_out]
    sent = local_call(functools.partial(out_kernel, True), out_shape, out_inputs, scalars=1)
    came = shift(sent, "c", 1)
    kept = local_call(functools.partial(out_kernel, False), out_shape, out_inputs, scalars=1)
    arrived = lax.all_to_all(
        (kept.astype(F32) + came.astype(F32)).astype(BF), PLANE, 0, 0, tiled=True
    )
    stream, down_part = local_call(
        down_kernel,
        [
            jax.ShapeDtypeStruct((rows_each, w_in.shape[1]), BF),
            jax.ShapeDtypeStruct((n_head, rows_each // 2 + LONGEST, LANES), BF),
        ],
        [info, arrived, own_embed, down_here],
        scalars=1,
    )
    states = lax.all_to_all(down_part, HEAD, 0, 0, tiled=True)
    n_skip = lax.axis_size(SKIP)
    states = local_call(
        sum_kernel, jax.ShapeDtypeStruct((n_skip, *states.shape[1:]), BF), [states]
    )
    states = lax.all_to_all(states, SKIP, 0, 0, tiled=True)
    others = shift(states, "zp", 1)
    by_source = slot_patch.reshape(-1, 2, n_yl, rows_each).transpose(1, 0, 2, 3)
    by_source = by_source.reshape(2, n_skip, rows_each)
    labels_main = by_source.reshape(2, n_skip, 2, -1).transpose(0, 2, 1, 3).reshape(2, 2, -1)
    labels_rest = by_source.reshape(2, n_skip, -1, LONGEST).transpose(0, 2, 1, 3)
    labels_rest = labels_rest.reshape(2, rows_each // LONGEST, -1)
    capacity = bytes_here + LANES
    room = [
        pltpu.VMEM((n_skip * rows_each // 2, LANES), BF),
        pltpu.VMEM((n_skip * LONGEST, LANES), BF),
    ]
    near = local_call(
        near_kernel,
        jax.ShapeDtypeStruct((capacity, LANES), F32),
        [info, labels_main, labels_rest, states],
        scratch=room,
        scalars=1,
    )
    byte_out = local_call(
        cross_kernel,
        jax.ShapeDtypeStruct((cross_size, bytes_here), BF),
        [info, labels_main, labels_rest, patch_ids[None, :], rows, others, near],
        scratch=[pltpu.VMEM((capacity, LANES), F32), *room],
        scalars=1,
    ).T
    return (stream, byte_out)


def solution(mesh):
    torus = Mesh(
        mesh.devices.reshape(4, 2, 2, 2, 2, 4, 2), ("zh", "zm", "zp", "yl", "yh", "x", "c")
    )
    return jax.shard_map(
        layer,
        mesh=torus,
        in_specs=(
            P(SEQ, HEAD),
            P(SEQ),
            P(),
            P(),
            P(SEQ, HEAD),
            P(),
            P(SEQ, None, HEAD),
            P(HEAD, None),
            P(HEAD, SEQ),
        ),
        out_specs=(P(SEQ, HEAD), P(SEQ, HEAD)),
        check_vma=False,
    )
```

```python
import functools
import math

import jax
import jax.numpy as jnp
from jax import lax
from jax.experimental import pallas as pl
from jax.experimental.pallas import tpu as pltpu
from jax.sharding import Mesh
from jax.sharding import PartitionSpec as P


HEAD_SIZE = 128
WINDOW = 8
LONGEST = 16
ZL = ("zm", "zp")
Z = ("zh", "zm", "zp")
SEQ = ("zh", "zm", "zp", "yl")
SKIP = ("zh", "zm", "yl")
PLANE = ("yl", "yh", "x")
HEAD = ("yh", "x", "c")
EPSILON = 1e-05
FLOOR_SCORE = -1e30
BF = jnp.bfloat16
F32 = jnp.float32
MAIN = 64
LANES = 128


VMEM = pl.BlockSpec(memory_space=pltpu.VMEM)
SMEM = pl.BlockSpec(memory_space=pltpu.SMEM)


def local_call(kernel, out, inputs, scratch=(), scalars=0, last=(), flops=10**8, moved=10**6):
    specs = [SMEM] * scalars + [VMEM] * (len(inputs) - scalars - len(last)) + list(last)
    many = isinstance(out, (list, tuple))
    return pl.pallas_call(
        kernel,
        out_shape=out,
        grid=(1,) if last else (),
        in_specs=specs,
        out_specs=[VMEM] * len(out) if many else VMEM,
        scratch_shapes=list(scratch),
        compiler_params=pltpu.CompilerParams(vmem_limit_bytes=48 << 20),
        cost_estimate=pl.CostEstimate(flops=flops, bytes_accessed=moved, transcendentals=0),
    )(*inputs)


def matmul(a, b):
    return lax.dot_general(a, b, (((1,), (0,)), ((), ())), preferred_element_type=F32)


def matmul_t(a, b):
    return lax.dot_general(a, b, (((1,), (1,)), ((), ())), preferred_element_type=F32)


def split_kernel(w_in, out):
    width = out.shape[2]
    for i in range(out.shape[0]):
        out[i] = w_in[:, (i % 2) * width : (i % 2 + 1) * width]


def take_kernel(weights, out):
    out[...] = weights[...]


def pool_kernel(flip, info, slots, ids, rows, out):
    blocks, packed_rows, _ = out.shape
    count = slots.shape[0] // (2 * blocks)
    half = count // 2
    group = packed_rows - half
    blank = jnp.zeros((group, LANES - group * (count // group)), F32)
    side = 1 - info[1] if flip else info[1]

    def step(i, unused):
        at = pl.multiple_of((2 * i + side) * count, count)
        match = jnp.where(slots[pl.ds(at, count), :] == ids[...], 1.0, 0.0).astype(BF)
        part = matmul_t(match, rows[...])
        out[i, 0:half, 0:MAIN] = part[0:half, 0:MAIN].astype(BF)
        out[i, 0:half, MAIN:LANES] = part[half:count, 0:MAIN].astype(BF)
        rest = [part[group * g : group * (g + 1), MAIN:] for g in range(count // group)]
        out[i, half:packed_rows, :] = jnp.concatenate(rest + [blank], axis=1).astype(BF)
        return unused

    lax.fori_loop(0, blocks, step, 0, unroll=4)


def sum_kernel(arrived, out):
    total = jnp.zeros(arrived.shape[1:], F32)
    for i in range(arrived.shape[0]):
        total = total + arrived[i].astype(F32)
    held = total.astype(BF)
    for i in range(out.shape[0]):
        out[i] = held


def embed_kernel(info, pooled, gain, near, far, out, keep):
    heads, count, size = keep.shape
    each = count // 2
    half = each // 2
    spare = size - MAIN
    group = pooled.shape[1] - half
    square = jnp.zeros((count, 1), F32)
    for h in range(heads):
        two = [pooled[y * heads + h].astype(F32) for y in range(2)]
        main = [v[0:half, at : at + MAIN] for v in two for at in (0, MAIN)]
        main = jnp.concatenate(main, axis=0)
        rest = [v[half:, spare * g : spare * (g + 1)] for v in two for g in range(each // group)]
        rest = jnp.concatenate(rest, axis=0)
        keep[h, :, 0:MAIN] = main
        keep[h, :, MAIN:size] = rest
        square = square + jnp.sum(main * main, axis=1, keepdims=True)
        square = square + jnp.sum(rest * rest, axis=1, keepdims=True)
    scale = lax.rsqrt(square / (heads * size) + EPSILON)
    total = jnp.zeros(out.shape[1:], F32)
    for k in range(heads // 2):
        for source, h in ((near, 2 * k + info[5]), (far, 2 * k + 1 - info[5])):
            normed = keep[h] * scale * gain[pl.ds(h, 1), :]
            total = total + matmul(normed.astype(BF), source[k * size : (k + 1) * size, :])
    held = total.astype(BF)
    for i in range(out.shape[0]):
        out[i] = held


def project_kernel(info, own, other, gain, weights, queries, kv):
    planes = own.shape[0] // 2
    count, width = own.shape[1:]
    size = 2 * width
    columns = 3 * HEAD_SIZE
    square = jnp.zeros((count, width), F32)
    for source in (own, other):
        for b in range(2 * planes):
            wide = source[b].astype(F32)
            square = square + wide * wide
    square = jnp.sum(square, axis=1, keepdims=True)
    scale = lax.rsqrt(square / (2 * planes * size) + EPSILON)
    total = jnp.zeros((count, columns), F32)
    for side, source in ((0, own), (1, other)):
        core = info[0] if side == 0 else 1 - info[0]
        for p in range(planes):
            h = 2 * p + core
            both = jnp.concatenate([source[p], source[planes + p]], axis=1).astype(F32)
            attn_in = both * scale * gain[pl.ds(h, 1), :]
            at = pl.multiple_of(h * size, size)
            total = total + matmul(attn_in.astype(BF), weights[pl.ds(at, size), :])
    queries[...] = total[:, 0:HEAD_SIZE].astype(BF)
    held = total[:, HEAD_SIZE:].astype(BF)
    for i in range(kv.shape[0]):
        kv[i] = held


def attend_kernel(info, queries, slots, labels, *rest):
    pieces, out, scores = rest[:-2], rest[-2], rest[-1]
    query = queries[...]
    own = pl.multiple_of(info[4] * query.shape[0], query.shape[0])
    mine = slots[pl.ds(own, query.shape[0]), :]
    peak = jnp.full((query.shape[0], 1), FLOOR_SCORE, F32)
    turns = ((0, 0), (3, 0), (1, 0), (2, 0), (2, labels.shape[1] // 2))
    start = 0
    for piece, (turn, at) in zip(pieces, turns):
        size = piece.shape[0]
        here = labels[pl.ds((info[3] + turn) % 4, 1), at : at + size]
        part = matmul_t(query, piece[:, 0:HEAD_SIZE]) * (1.0 / math.sqrt(HEAD_SIZE))
        part = jnp.where(here <= mine, part, FLOOR_SCORE)
        scores[:, start : start + size] = part
        peak = jnp.maximum(peak, jnp.max(part, axis=1, keepdims=True))
        start += size
    total = jnp.zeros_like(peak)
    mixed = jnp.zeros(query.shape, F32)
    start = 0
    for piece in pieces:
        size = piece.shape[0]
        weights = jnp.exp(scores[:, start : start + size] - peak)
        total = total + jnp.sum(weights, axis=1, keepdims=True)
        mixed = mixed + matmul(weights.astype(BF), piece[:, HEAD_SIZE:])
        start += size
    out[...] = (mixed / total).astype(BF)


def out_kernel(flip, info, attended, w_out, out):
    count, width = out.shape[1:]
    planes = out.shape[0] // 2
    mine = attended[...]
    at = pl.multiple_of(info[1] * HEAD_SIZE, HEAD_SIZE)
    core = 1 - info[0] if flip else info[0]
    for p in range(planes):
        cols = pl.multiple_of((2 * p + core) * width, width)
        part = matmul(mine, w_out[pl.ds(at, HEAD_SIZE), pl.ds(cols, width)]).astype(BF)
        out[p] = part[0:count]
        out[planes + p] = part[count:]


def down_kernel(info, arrived, embed, w_down, stream, out):
    count, width = stream.shape
    half = count // 2
    planes = embed.shape[0] // 2
    size = MAIN + LONGEST
    at = pl.multiple_of(info[1] * count, count)
    low = embed[info[2], pl.ds(at, count), :]
    high = embed[planes + info[2], pl.ds(at, count), :]
    total = jnp.concatenate([low, high], axis=1).astype(F32)
    added = jnp.zeros(total.shape, F32)
    for h in range(arrived.shape[0]):
        added = added + arrived[h].astype(F32)
    held = (total + added).astype(BF)
    stream[...] = held
    group = out.shape[1] - half
    blank = jnp.zeros((group, LANES - LONGEST * (count // group)), F32)
    for h in range(out.shape[0]):
        part = matmul(held, w_down[h * width : (h + 1) * width, :])
        out[h, 0:half, 0:MAIN] = part[0:half, 0:MAIN].astype(BF)
        out[h, 0:half, MAIN:LANES] = part[half:, 0:MAIN].astype(BF)
        rest = [part[group * g : group * (g + 1), MAIN:size] for g in range(count // group)]
        out[h, half:, :] = jnp.concatenate(rest + [blank], axis=1).astype(BF)


def pick_rows(base, labels_main, labels_rest, states, main, rest, put):
    groups = labels_rest.shape[0]
    half = groups * LONGEST // 2
    for i in range(states.shape[0]):
        main[i * half : (i + 1) * half, :] = states[i, 0:half, :]
        rest[i * LONGEST : (i + 1) * LONGEST, :] = states[i, half:, :]
    step = LANES

    def hot(at, label):
        wanted = base + at + lax.broadcasted_iota(jnp.int32, (step, label.shape[1]), 0)
        return jnp.where(wanted == label, 1.0, 0.0).astype(BF)

    def pick(i, unused):
        at = pl.multiple_of(i * step, step)
        low = matmul(hot(at, labels_main[0:1, :]), main[...])
        high = matmul(hot(at, labels_main[1:2, :]), main[...])
        tail = jnp.zeros((step, LONGEST), F32)
        for g in range(groups):
            here = matmul(hot(at, labels_rest[g : g + 1, :]), rest[...])
            tail = tail + here[:, g * LONGEST : (g + 1) * LONGEST]
        put(at, low[:, 0:MAIN] + high[:, MAIN:LANES], tail)
        return unused

    return pick


def near_kernel(info, labels_main, labels_rest, states, out, main, rest):
    group = info[5]

    def put(at, low, tail):
        blank = jnp.zeros((LANES, LANES - MAIN - LONGEST), F32)
        out[pl.ds(at, LANES), :] = jnp.concatenate([low, tail, blank], axis=1)

    pick = pick_rows(
        info[6], labels_main.at[group], labels_rest.at[group], states, main, rest, put
    )
    lax.fori_loop(0, out.shape[0] // LANES, pick, 0, unroll=True)


def cross_kernel(
    info, labels_main, labels_rest, ids, rows, states, near, out, picked, main, rest
):
    size = rows.shape[0]
    group = 1 - info[5]
    base = info[6]

    def put(at, low, tail):
        blank = jnp.zeros((LANES, LANES - MAIN - LONGEST), F32)
        here = jnp.concatenate([low, tail, blank], axis=1)
        picked[pl.ds(at, LANES), :] = near[pl.ds(at, LANES), :] + here

    pick = pick_rows(base, labels_main.at[group], labels_rest.at[group], states, main, rest, put)
    lax.fori_loop(0, near.shape[0] // LANES, pick, 0, unroll=True)
    keys = picked[...].astype(BF)[:, 0:size]
    turned = picked[...].T.astype(BF)
    wanted = base + lax.broadcasted_iota(jnp.int32, (near.shape[0], LANES), 0)
    allowed = wanted >= 0

    for i in range(rows.shape[1] // LANES):
        at = slice(i * LANES, (i + 1) * LANES)
        mine = rows[:, at]
        far = ids[:, at] - wanted
        close = (far >= 0) & (far < WINDOW) & allowed
        scores = matmul(keys, mine) * (1.0 / math.sqrt(size))
        scores = jnp.where(close, scores, FLOOR_SCORE)
        weights = jnp.exp(scores - jnp.max(scores, axis=0, keepdims=True))
        total = jnp.sum(weights, axis=0, keepdims=True)
        reached = matmul(turned, weights.astype(BF))[0:size] / total
        out[:, at] = (mine.astype(F32) + reached).astype(BF)


def shift(x, axis, by):
    n = lax.axis_size(axis)
    return lax.ppermute(x, axis, [(i, (i + by) % n) for i in range(n)])


def over_plane(copies):
    near = lax.all_to_all(copies, PLANE, 0, 0, tiled=True)
    return near, shift(near, "c", 1)


def over_z(four):
    half = four.shape[0] // 2
    after = shift(four, Z, 1)
    before = shift(four, Z, -1)
    return [four, after, before, shift(four[:half], Z, 2), shift(four[half:], Z, -2)]


def layer(byte_states, patch_ids, slot_patch, pool_gain, w_in, attn_gain, w_qkv, w_out, w_down):
    n_z = lax.axis_size(Z)
    n_zl = lax.axis_size(ZL)
    n_yl = lax.axis_size("yl")
    n_head = lax.axis_size(HEAD)
    patches = slot_patch.shape[0]
    rows_z = patches // n_z
    rows_each = rows_z // n_yl
    bytes_here, cross_size = byte_states.shape
    info = jnp.stack(
        [
            lax.axis_index("c"),
            lax.axis_index("yl"),
            lax.axis_index(("yh", "x")),
            lax.axis_index(ZL),
            lax.axis_index(Z),
            lax.axis_index("zp"),
            patch_ids[0] - (WINDOW - 1),
        ]
    ).astype(jnp.int32)
    n_plane = lax.axis_size(PLANE)
    slots = slot_patch[:, None]
    rows = byte_states.T
    first = info[1] == 0

    w_in_parts = local_call(
        split_kernel,
        jax.ShapeDtypeStruct((n_z, w_in.shape[0], w_in.shape[1] // n_yl), BF),
        [w_in],
    )
    w_in_near = lax.all_to_all(w_in_parts, SKIP, 0, 0, tiled=True)
    w_in_near = w_in_near.reshape(-1, w_in_parts.shape[2])
    w_in_far = shift(w_in_near, "zp", 1)

    halves = [
        jnp.concatenate([w_qkv[:, j, k * HEAD_SIZE : (k + 1) * HEAD_SIZE] for j in range(3)], axis=1)
        for k in range(n_yl)
    ]
    depth = w_qkv.shape[0]
    down_pieces = [w_down[:depth], w_down[depth:]]
    sent = jnp.concatenate([jnp.where(first, halves[1], halves[0]), *down_pieces], axis=1)
    came = shift(sent, "yl", 1)
    kept = jnp.concatenate([jnp.where(first, halves[0], halves[1]), *down_pieces], axis=1)
    low = jnp.where(first, kept, came)
    high = jnp.where(first, came, kept)
    wide = halves[0].shape[1]
    part = w_down.shape[1]
    down_both = [
        jnp.concatenate([v[:, wide : wide + part], v[:, wide + part :]], axis=0) for v in (low, high)
    ]
    blank = jnp.zeros((2 * depth, LANES - 2 * part), BF)
    mine = jnp.concatenate([low[:, :wide], high[:, :wide]], axis=0)
    weights = lax.all_gather(
        jnp.concatenate([mine, *down_both, blank], axis=1), Z, axis=0, tiled=True
    )

    packed = jax.ShapeDtypeStruct((n_z, rows_each // 2 + LONGEST, LANES), BF)
    pool_inputs = [info, slots, patch_ids[None, :], rows]
    sent = local_call(functools.partial(pool_kernel, True), packed, pool_inputs, scalars=1)
    came = shift(sent, "yl", 1)
    kept = local_call(functools.partial(pool_kernel, False), packed, pool_inputs, scalars=1)
    pooled = (kept.astype(F32) + came.astype(F32)).astype(BF)
    pooled = lax.all_to_all(pooled, Z, 0, 0, tiled=True)
    pooled = local_call(
        sum_kernel, jax.ShapeDtypeStruct((2 * n_plane, *pooled.shape[1:]), BF), [pooled]
    )
    pooled = lax.all_to_all(pooled, (*PLANE, "c"), 0, 0, tiled=True)
    embed = local_call(
        embed_kernel,
        jax.ShapeDtypeStruct((n_plane, rows_z, w_in_near.shape[1]), BF),
        [info, pooled, pool_gain.reshape(n_head, cross_size), w_in_near, w_in_far],
        scratch=[pltpu.VMEM((n_head, rows_z, cross_size), F32)],
        scalars=1,
    )
    own_embed, other_embed = over_plane(embed)
    queries, kv = local_call(
        project_kernel,
        [
            jax.ShapeDtypeStruct((rows_z, HEAD_SIZE), BF),
            jax.ShapeDtypeStruct((n_z // n_zl, rows_z, 2 * HEAD_SIZE), BF),
        ],
        [info, own_embed, other_embed, attn_gain.reshape(n_head, -1), weights],
        scalars=1,
        last=[pl.BlockSpec((weights.shape[0], wide), lambda i: (0, 0))],
    )
    down_here = local_call(
        take_kernel,
        jax.ShapeDtypeStruct((weights.shape[0], LANES), BF),
        [weights],
        last=[pl.BlockSpec((weights.shape[0], LANES), lambda i: (0, wide // LANES))],
    )
    labels = slot_patch.reshape(n_z // n_zl, n_zl, rows_z).transpose(1, 0, 2).reshape(n_zl, -1)
    kv = lax.all_to_all(kv, "zh", 0, 0, tiled=True).reshape(-1, kv.shape[2])
    attended = local_call(
        attend_kernel,
        jax.ShapeDtypeStruct((rows_z, HEAD_SIZE), BF),
        [info, queries, slots, labels, *over_z(kv)],
        scratch=[pltpu.VMEM((rows_z, patches), F32)],
        scalars=1,
    )
    out_shape = jax.ShapeDtypeStruct((n_plane, rows_each, w_out.shape[1] // n_head), BF)
    out_inputs = [info, attended, w_out]
    sent = local_call(functools.partial(out_kernel, True), out_shape, out_inputs, scalars=1)
    came = shift(sent, "c", 1)
    kept = local_call(functools.partial(out_kernel, False), out_shape, out_inputs, scalars=1)
    arrived = lax.all_to_all(
        (kept.astype(F32) + came.astype(F32)).astype(BF), PLANE, 0, 0, tiled=True
    )
    stream, down_part = local_call(
        down_kernel,
        [
            jax.ShapeDtypeStruct((rows_each, w_in.shape[1]), BF),
            jax.ShapeDtypeStruct((n_head, rows_each // 2 + LONGEST, LANES), BF),
        ],
        [info, arrived, own_embed, down_here],
        scalars=1,
    )
    states = lax.all_to_all(down_part, HEAD, 0, 0, tiled=True)
    n_skip = lax.axis_size(SKIP)
    states = local_call(
        sum_kernel, jax.ShapeDtypeStruct((n_skip, *states.shape[1:]), BF), [states]
    )
    states = lax.all_to_all(states, SKIP, 0, 0, tiled=True)
    others = shift(states, "zp", 1)
    by_source = slot_patch.reshape(-1, 2, n_yl, rows_each).transpose(1, 0, 2, 3)
    by_source = by_source.reshape(2, n_skip, rows_each)
    labels_main = by_source.reshape(2, n_skip, 2, -1).transpose(0, 2, 1, 3).reshape(2, 2, -1)
    labels_rest = by_source.reshape(2, n_skip, -1, LONGEST).transpose(0, 2, 1, 3)
    labels_rest = labels_rest.reshape(2, rows_each // LONGEST, -1)
    capacity = bytes_here + LANES
    room = [
        pltpu.VMEM((n_skip * rows_each // 2, LANES), BF),
        pltpu.VMEM((n_skip * LONGEST, LANES), BF),
    ]
    near = local_call(
        near_kernel,
        jax.ShapeDtypeStruct((capacity, LANES), F32),
        [info, labels_main, labels_rest, states],
        scratch=room,
        scalars=1,
    )
    byte_out = local_call(
        cross_kernel,
        jax.ShapeDtypeStruct((cross_size, bytes_here), BF),
        [info, labels_main, labels_rest, patch_ids[None, :], rows, others, near],
        scratch=[pltpu.VMEM((capacity, LANES), F32), *room],
        scalars=1,
    ).T
    return (stream, byte_out)


def solution(mesh):
    torus = Mesh(
        mesh.devices.reshape(4, 2, 2, 2, 2, 4, 2), ("zh", "zm", "zp", "yl", "yh", "x", "c")
    )
    return jax.shard_map(
        layer,
        mesh=torus,
        in_specs=(
            P(SEQ, HEAD),
            P(SEQ),
            P(),
            P(),
            P(SEQ, HEAD),
            P(),
            P(SEQ, None, HEAD),
            P(HEAD, None),
            P(HEAD, SEQ),
        ),
        out_specs=(P(SEQ, HEAD), P(SEQ, HEAD)),
        check_vma=False,
    )
```

```python
import functools
import math

import jax
import jax.numpy as jnp
from jax import lax
from jax.experimental import pallas as pl
from jax.experimental.pallas import tpu as pltpu
from jax.sharding import Mesh
from jax.sharding import PartitionSpec as P


HEAD_SIZE = 128
WINDOW = 8
LONGEST = 16
ZL = ("zm", "zp")
Z = ("zh", "zm", "zp")
SEQ = ("zh", "zm", "zp", "yl")
SKIP = ("zh", "zm", "yl")
PLANE = ("yl", "yh", "x")
HEAD = ("yh", "x", "c")
EPSILON = 1e-05
FLOOR_SCORE = -1e30
BF = jnp.bfloat16
F32 = jnp.float32
MAIN = 64
LANES = 128


VMEM = pl.BlockSpec(memory_space=pltpu.VMEM)
SMEM = pl.BlockSpec(memory_space=pltpu.SMEM)


def local_call(kernel, out, inputs, scratch=(), scalars=0, last=(), room=48, flops=10**8, moved=10**6):
    specs = [SMEM] * scalars + [VMEM] * (len(inputs) - scalars - len(last)) + list(last)
    many = isinstance(out, (list, tuple))
    return pl.pallas_call(
        kernel,
        out_shape=out,
        grid=(1,) if last else (),
        in_specs=specs,
        out_specs=[VMEM] * len(out) if many else VMEM,
        scratch_shapes=list(scratch),
        compiler_params=pltpu.CompilerParams(vmem_limit_bytes=room << 20),
        cost_estimate=pl.CostEstimate(flops=flops, bytes_accessed=moved, transcendentals=0),
    )(*inputs)


def matmul(a, b):
    return lax.dot_general(a, b, (((1,), (0,)), ((), ())), preferred_element_type=F32)


def matmul_t(a, b):
    return lax.dot_general(a, b, (((1,), (1,)), ((), ())), preferred_element_type=F32)


def split_kernel(w_in, out):
    width = out.shape[2]
    for i in range(out.shape[0]):
        out[i] = w_in[:, (i % 2) * width : (i % 2 + 1) * width]


def take_kernel(weights, out, arrived):
    count = weights.shape[1]
    copy = pltpu.make_async_copy(weights.at[:, count - LANES : count], out, arrived)
    copy.start()
    copy.wait()


def pool_kernel(flip, info, slots, ids, rows, out):
    blocks, packed_rows, _ = out.shape
    count = slots.shape[0] // (2 * blocks)
    half = count // 2
    group = packed_rows - half
    blank = jnp.zeros((group, LANES - group * (count // group)), F32)
    side = 1 - info[1] if flip else info[1]

    def step(i, unused):
        at = pl.multiple_of((2 * i + side) * count, count)
        match = jnp.where(slots[pl.ds(at, count), :] == ids[...], 1.0, 0.0).astype(BF)
        part = matmul_t(match, rows[...])
        out[i, 0:half, 0:MAIN] = part[0:half, 0:MAIN].astype(BF)
        out[i, 0:half, MAIN:LANES] = part[half:count, 0:MAIN].astype(BF)
        rest = [part[group * g : group * (g + 1), MAIN:] for g in range(count // group)]
        out[i, half:packed_rows, :] = jnp.concatenate(rest + [blank], axis=1).astype(BF)
        return unused

    lax.fori_loop(0, blocks, step, 0, unroll=4)


def sum_kernel(arrived, out):
    total = jnp.zeros(arrived.shape[1:], F32)
    for i in range(arrived.shape[0]):
        total = total + arrived[i].astype(F32)
    held = total.astype(BF)
    for i in range(out.shape[0]):
        out[i] = held


def embed_kernel(pooled, gain, w_in, out, keep):
    heads, count, size = keep.shape
    each = count // 2
    half = each // 2
    spare = size - MAIN
    group = pooled.shape[1] - half
    square = jnp.zeros((count, 1), F32)
    for h in range(heads):
        two = [pooled[y * heads + h].astype(F32) for y in range(2)]
        main = [v[0:half, at : at + MAIN] for v in two for at in (0, MAIN)]
        main = jnp.concatenate(main, axis=0)
        rest = [v[half:, spare * g : spare * (g + 1)] for v in two for g in range(each // group)]
        rest = jnp.concatenate(rest, axis=0)
        keep[h, :, 0:MAIN] = main
        keep[h, :, MAIN:size] = rest
        square = square + jnp.sum(main * main, axis=1, keepdims=True)
        square = square + jnp.sum(rest * rest, axis=1, keepdims=True)
    scale = lax.rsqrt(square / (heads * size) + EPSILON)
    total = jnp.zeros(out.shape[1:], F32)
    for h in range(heads):
        normed = keep[h] * scale * gain[h : h + 1, :]
        total = total + matmul(normed.astype(BF), w_in[h * size : (h + 1) * size, :])
    held = total.astype(BF)
    for i in range(out.shape[0]):
        out[i] = held


def project_kernel(info, own, other, gain, weights, queries, kv):
    planes = own.shape[0] // 2
    count, width = own.shape[1:]
    size = 2 * width
    columns = 3 * HEAD_SIZE
    square = jnp.zeros((count, width), F32)
    for source in (own, other):
        for b in range(2 * planes):
            wide = source[b].astype(F32)
            square = square + wide * wide
    square = jnp.sum(square, axis=1, keepdims=True)
    scale = lax.rsqrt(square / (2 * planes * size) + EPSILON)
    total = jnp.zeros((count, columns), F32)
    for side, source in ((0, own), (1, other)):
        core = info[0] if side == 0 else 1 - info[0]
        for p in range(planes):
            h = 2 * p + core
            both = jnp.concatenate([source[p], source[planes + p]], axis=1).astype(F32)
            attn_in = both * scale * gain[pl.ds(h, 1), :]
            at = pl.multiple_of(h * size, size)
            total = total + matmul(attn_in.astype(BF), weights[pl.ds(at, size), :])
    queries[...] = total[:, 0:HEAD_SIZE].astype(BF)
    held = total[:, HEAD_SIZE:].astype(BF)
    for i in range(kv.shape[0]):
        kv[i] = held


def attend_kernel(info, queries, slots, labels, *rest):
    pieces, out, scores = rest[:-2], rest[-2], rest[-1]
    query = queries[...]
    own = pl.multiple_of(info[4] * query.shape[0], query.shape[0])
    mine = slots[pl.ds(own, query.shape[0]), :]
    peak = jnp.full((query.shape[0], 1), FLOOR_SCORE, F32)
    turns = ((0, 0), (3, 0), (1, 0), (2, 0), (2, 2))
    start = 0
    for piece, (turn, first) in zip(pieces, turns):
        size = piece.shape[0]
        column = (info[3] + turn) % 4
        here = [
            labels[pl.ds(4 * (first + i) + column, 1), :] for i in range(size // labels.shape[1])
        ]
        here = jnp.concatenate(here, axis=1)
        part = matmul_t(query, piece[:, 0:HEAD_SIZE]) * (1.0 / math.sqrt(HEAD_SIZE))
        part = jnp.where(here <= mine, part, FLOOR_SCORE)
        scores[:, start : start + size] = part
        peak = jnp.maximum(peak, jnp.max(part, axis=1, keepdims=True))
        start += size
    total = jnp.zeros_like(peak)
    mixed = jnp.zeros(query.shape, F32)
    start = 0
    for piece in pieces:
        size = piece.shape[0]
        weights = jnp.exp(scores[:, start : start + size] - peak)
        total = total + jnp.sum(weights, axis=1, keepdims=True)
        mixed = mixed + matmul(weights.astype(BF), piece[:, HEAD_SIZE:])
        start += size
    out[...] = (mixed / total).astype(BF)


def out_kernel(flip, info, attended, w_out, out):
    count, width = out.shape[1:]
    planes = out.shape[0] // 2
    mine = attended[...]
    at = pl.multiple_of(info[1] * HEAD_SIZE, HEAD_SIZE)
    core = 1 - info[0] if flip else info[0]
    for p in range(planes):
        cols = pl.multiple_of((2 * p + core) * width, width)
        part = matmul(mine, w_out[pl.ds(at, HEAD_SIZE), pl.ds(cols, width)]).astype(BF)
        out[p] = part[0:count]
        out[planes + p] = part[count:]


def down_kernel(info, arrived, embed, w_down, stream, out):
    count, width = stream.shape
    half = count // 2
    planes = embed.shape[0] // 2
    size = MAIN + LONGEST
    at = pl.multiple_of(info[1] * count, count)
    low = embed[info[2], pl.ds(at, count), :]
    high = embed[planes + info[2], pl.ds(at, count), :]
    total = jnp.concatenate([low, high], axis=1).astype(F32)
    added = jnp.zeros(total.shape, F32)
    for h in range(arrived.shape[0]):
        added = added + arrived[h].astype(F32)
    held = (total + added).astype(BF)
    stream[...] = held
    group = out.shape[1] - half
    blank = jnp.zeros((group, LANES - LONGEST * (count // group)), F32)
    for h in range(out.shape[0]):
        part = matmul(held, w_down[h * width : (h + 1) * width, :])
        out[h, 0:half, 0:MAIN] = part[0:half, 0:MAIN].astype(BF)
        out[h, 0:half, MAIN:LANES] = part[half:, 0:MAIN].astype(BF)
        rest = [part[group * g : group * (g + 1), MAIN:size] for g in range(count // group)]
        out[h, half:, :] = jnp.concatenate(rest + [blank], axis=1).astype(BF)


def pick_rows(base, labels_main, labels_rest, states, main, rest, put):
    groups = labels_rest.shape[0]
    half = groups * LONGEST // 2
    for i in range(states.shape[0]):
        main[i * half : (i + 1) * half, :] = states[i, 0:half, :]
        rest[i * LONGEST : (i + 1) * LONGEST, :] = states[i, half:, :]
    step = LANES

    def hot(at, label):
        wanted = base + at + lax.broadcasted_iota(jnp.int32, (step, label.shape[1]), 0)
        return jnp.where(wanted == label, 1.0, 0.0).astype(BF)

    def pick(i, unused):
        at = pl.multiple_of(i * step, step)
        low = matmul(hot(at, labels_main[0:1, :]), main[...])
        high = matmul(hot(at, labels_main[1:2, :]), main[...])
        tail = jnp.zeros((step, LONGEST), F32)
        for g in range(groups):
            here = matmul(hot(at, labels_rest[g : g + 1, :]), rest[...])
            tail = tail + here[:, g * LONGEST : (g + 1) * LONGEST]
        put(at, low[:, 0:MAIN] + high[:, MAIN:LANES], tail)
        return unused

    return pick


def near_kernel(info, labels_main, labels_rest, states, out, main, rest):
    group = info[5]

    def put(at, low, tail):
        blank = jnp.zeros((LANES, LANES - MAIN - LONGEST), F32)
        out[pl.ds(at, LANES), :] = jnp.concatenate([low, tail, blank], axis=1)

    pick = pick_rows(
        info[6], labels_main.at[group], labels_rest.at[group], states, main, rest, put
    )
    lax.fori_loop(0, out.shape[0] // LANES, pick, 0, unroll=True)


def cross_kernel(
    info, labels_main, labels_rest, ids, rows, states, near, out, picked, main, rest
):
    size = rows.shape[0]
    group = 1 - info[5]
    base = info[6]

    def put(at, low, tail):
        blank = jnp.zeros((LANES, LANES - MAIN - LONGEST), F32)
        here = jnp.concatenate([low, tail, blank], axis=1)
        picked[pl.ds(at, LANES), :] = near[pl.ds(at, LANES), :] + here

    pick = pick_rows(base, labels_main.at[group], labels_rest.at[group], states, main, rest, put)
    lax.fori_loop(0, near.shape[0] // LANES, pick, 0, unroll=True)
    keys = picked[...].astype(BF)[:, 0:size]
    turned = picked[...].T.astype(BF)
    wanted = base + lax.broadcasted_iota(jnp.int32, (near.shape[0], LANES), 0)
    allowed = wanted >= 0

    for i in range(rows.shape[1] // LANES):
        at = slice(i * LANES, (i + 1) * LANES)
        mine = rows[:, at]
        far = ids[:, at] - wanted
        close = (far >= 0) & (far < WINDOW) & allowed
        scores = matmul(keys, mine) * (1.0 / math.sqrt(size))
        scores = jnp.where(close, scores, FLOOR_SCORE)
        weights = jnp.exp(scores - jnp.max(scores, axis=0, keepdims=True))
        total = jnp.sum(weights, axis=0, keepdims=True)
        reached = matmul(turned, weights.astype(BF))[0:size] / total
        out[:, at] = (mine.astype(F32) + reached).astype(BF)


def shift(x, axis, by):
    n = lax.axis_size(axis)
    return lax.ppermute(x, axis, [(i, (i + by) % n) for i in range(n)])


def over_plane(copies):
    near = lax.all_to_all(copies, PLANE, 0, 0, tiled=True)
    return near, shift(near, "c", 1)


def over_z(four):
    half = four.shape[0] // 2
    after = shift(four, Z, 1)
    before = shift(four, Z, -1)
    return [four, after, before, shift(four[:half], Z, 2), shift(four[half:], Z, -2)]


def layer(byte_states, patch_ids, slot_patch, pool_gain, w_in, attn_gain, w_qkv, w_out, w_down):
    n_z = lax.axis_size(Z)
    n_zl = lax.axis_size(ZL)
    n_yl = lax.axis_size("yl")
    n_head = lax.axis_size(HEAD)
    patches = slot_patch.shape[0]
    rows_z = patches // n_z
    rows_each = rows_z // n_yl
    bytes_here, cross_size = byte_states.shape
    info = jnp.stack(
        [
            lax.axis_index("c"),
            lax.axis_index("yl"),
            lax.axis_index(("yh", "x")),
            lax.axis_index(ZL),
            lax.axis_index(Z),
            lax.axis_index("zp"),
            patch_ids[0] - (WINDOW - 1),
        ]
    ).astype(jnp.int32)
    n_plane = lax.axis_size(PLANE)
    slots = slot_patch[:, None]
    rows = byte_states.T
    first = info[1] == 0

    w_in_parts = local_call(
        split_kernel,
        jax.ShapeDtypeStruct((n_z * n_yl, w_in.shape[0], w_in.shape[1] // n_yl), BF),
        [w_in],
    )
    w_in_here = lax.all_to_all(w_in_parts, SEQ, 0, 0, tiled=True)
    w_in_here = w_in_here.reshape(-1, w_in_parts.shape[2])

    halves = [
        jnp.concatenate([w_qkv[:, j, k * HEAD_SIZE : (k + 1) * HEAD_SIZE] for j in range(3)], axis=1)
        for k in range(n_yl)
    ]
    depth = w_qkv.shape[0]
    down_pieces = [w_down[:depth], w_down[depth:]]
    sent = jnp.concatenate([jnp.where(first, halves[1], halves[0]), *down_pieces], axis=1)
    came = shift(sent, "yl", 1)
    kept = jnp.concatenate([jnp.where(first, halves[0], halves[1]), *down_pieces], axis=1)
    low = jnp.where(first, kept, came)
    high = jnp.where(first, came, kept)
    wide = halves[0].shape[1]
    part = w_down.shape[1]
    down_both = [
        jnp.concatenate([v[:, wide : wide + part], v[:, wide + part :]], axis=0) for v in (low, high)
    ]
    blank = jnp.zeros((2 * depth, LANES - 2 * part), BF)
    mine = jnp.concatenate([low[:, :wide], high[:, :wide]], axis=0)
    weights = lax.all_gather(
        jnp.concatenate([mine, *down_both, blank], axis=1), Z, axis=0, tiled=True
    )

    packed = jax.ShapeDtypeStruct((n_z, rows_each // 2 + LONGEST, LANES), BF)
    pool_inputs = [info, slots, patch_ids[None, :], rows]
    sent = local_call(functools.partial(pool_kernel, True), packed, pool_inputs, scalars=1)
    came = shift(sent, "yl", 1)
    kept = local_call(functools.partial(pool_kernel, False), packed, pool_inputs, scalars=1)
    pooled = (kept.astype(F32) + came.astype(F32)).astype(BF)
    pooled = lax.all_to_all(pooled, Z, 0, 0, tiled=True)
    pooled = local_call(
        sum_kernel, jax.ShapeDtypeStruct((2 * n_plane, *pooled.shape[1:]), BF), [pooled]
    )
    pooled = lax.all_to_all(pooled, (*PLANE, "c"), 0, 0, tiled=True)
    embed = local_call(
        embed_kernel,
        jax.ShapeDtypeStruct((n_plane, rows_z, w_in_here.shape[1]), BF),
        [pooled, pool_gain.reshape(n_head, cross_size), w_in_here],
        scratch=[pltpu.VMEM((n_head, rows_z, cross_size), F32)],
    )
    own_embed, other_embed = over_plane(embed)
    queries, kv = local_call(
        project_kernel,
        [
            jax.ShapeDtypeStruct((rows_z, HEAD_SIZE), BF),
            jax.ShapeDtypeStruct((n_z // n_zl, rows_z, 2 * HEAD_SIZE), BF),
        ],
        [info, own_embed, other_embed, attn_gain.reshape(n_head, -1), weights],
        scalars=1,
        last=[pl.BlockSpec((weights.shape[0], wide), lambda i: (0, 0))],
    )
    down_here = local_call(
        take_kernel,
        jax.ShapeDtypeStruct((weights.shape[0], LANES), BF),
        [weights],
        scratch=[pltpu.SemaphoreType.DMA],
        last=[pl.BlockSpec(memory_space=pl.ANY)],
        room=60,
    )
    labels = slot_patch.reshape(n_z, rows_z)
    kv = lax.all_to_all(kv, "zh", 0, 0, tiled=True).reshape(-1, kv.shape[2])
    attended = local_call(
        attend_kernel,
        jax.ShapeDtypeStruct((rows_z, HEAD_SIZE), BF),
        [info, queries, slots, labels, *over_z(kv)],
        scratch=[pltpu.VMEM((rows_z, patches), F32)],
        scalars=1,
    )
    out_shape = jax.ShapeDtypeStruct((n_plane, rows_each, w_out.shape[1] // n_head), BF)
    out_inputs = [info, attended, w_out]
    sent = local_call(functools.partial(out_kernel, True), out_shape, out_inputs, scalars=1)
    came = shift(sent, "c", 1)
    kept = local_call(functools.partial(out_kernel, False), out_shape, out_inputs, scalars=1)
    arrived = lax.all_to_all(
        (kept.astype(F32) + came.astype(F32)).astype(BF), PLANE, 0, 0, tiled=True
    )
    stream, down_part = local_call(
        down_kernel,
        [
            jax.ShapeDtypeStruct((rows_each, w_in.shape[1]), BF),
            jax.ShapeDtypeStruct((n_head, rows_each // 2 + LONGEST, LANES), BF),
        ],
        [info, arrived, own_embed, down_here],
        scalars=1,
    )
    states = lax.all_to_all(down_part, HEAD, 0, 0, tiled=True)
    n_skip = lax.axis_size(SKIP)
    states = local_call(
        sum_kernel, jax.ShapeDtypeStruct((n_skip, *states.shape[1:]), BF), [states]
    )
    states = lax.all_to_all(states, SKIP, 0, 0, tiled=True)
    others = shift(states, "zp", 1)
    by_source = slot_patch.reshape(-1, 2, n_yl, rows_each).transpose(1, 0, 2, 3)
    by_source = by_source.reshape(2, n_skip, rows_each)
    labels_main = by_source.reshape(2, n_skip, 2, -1).transpose(0, 2, 1, 3).reshape(2, 2, -1)
    labels_rest = by_source.reshape(2, n_skip, -1, LONGEST).transpose(0, 2, 1, 3)
    labels_rest = labels_rest.reshape(2, rows_each // LONGEST, -1)
    capacity = bytes_here + LANES
    room = [
        pltpu.VMEM((n_skip * rows_each // 2, LANES), BF),
        pltpu.VMEM((n_skip * LONGEST, LANES), BF),
    ]
    near = local_call(
        near_kernel,
        jax.ShapeDtypeStruct((capacity, LANES), F32),
        [info, labels_main, labels_rest, states],
        scratch=room,
        scalars=1,
    )
    byte_out = local_call(
        cross_kernel,
        jax.ShapeDtypeStruct((cross_size, bytes_here), BF),
        [info, labels_main, labels_rest, patch_ids[None, :], rows, others, near],
        scratch=[pltpu.VMEM((capacity, LANES), F32), *room],
        scalars=1,
    ).T
    return (stream, byte_out)


def solution(mesh):
    torus = Mesh(
        mesh.devices.reshape(4, 2, 2, 2, 2, 4, 2), ("zh", "zm", "zp", "yl", "yh", "x", "c")
    )
    return jax.shard_map(
        layer,
        mesh=torus,
        in_specs=(
            P(SEQ, HEAD),
            P(SEQ),
            P(),
            P(),
            P(SEQ, HEAD),
            P(),
            P(SEQ, None, HEAD),
            P(HEAD, None),
            P(HEAD, SEQ),
        ),
        out_specs=(P(SEQ, HEAD), P(SEQ, HEAD)),
        check_vma=False,
    )
```

```python
import functools
import math

import jax
import jax.numpy as jnp
from jax import lax
from jax.experimental import pallas as pl
from jax.experimental.pallas import tpu as pltpu
from jax.sharding import Mesh
from jax.sharding import PartitionSpec as P


HEAD_SIZE = 128
WINDOW = 8
LONGEST = 16
ZL = ("zm", "zp")
Z = ("zh", "zm", "zp")
SEQ = ("zh", "zm", "zp", "yl")
SKIP = ("zh", "zm", "yl")
PLANE = ("yl", "yh", "x")
HEAD = ("yh", "x", "c")
EPSILON = 1e-05
FLOOR_SCORE = -1e30
BF = jnp.bfloat16
F32 = jnp.float32
MAIN = 64
LANES = 128


VMEM = pl.BlockSpec(memory_space=pltpu.VMEM)
SMEM = pl.BlockSpec(memory_space=pltpu.SMEM)


def local_call(kernel, out, inputs, scratch=(), scalars=0, last=(), flops=10**8, moved=10**6):
    specs = [SMEM] * scalars + [VMEM] * (len(inputs) - scalars - len(last)) + list(last)
    many = isinstance(out, (list, tuple))
    return pl.pallas_call(
        kernel,
        out_shape=out,
        grid=(1,) if last else (),
        in_specs=specs,
        out_specs=[VMEM] * len(out) if many else VMEM,
        scratch_shapes=list(scratch),
        compiler_params=pltpu.CompilerParams(vmem_limit_bytes=48 << 20),
        cost_estimate=pl.CostEstimate(flops=flops, bytes_accessed=moved, transcendentals=0),
    )(*inputs)


def matmul(a, b):
    return lax.dot_general(a, b, (((1,), (0,)), ((), ())), preferred_element_type=F32)


def matmul_t(a, b):
    return lax.dot_general(a, b, (((1,), (1,)), ((), ())), preferred_element_type=F32)


def split_kernel(w_in, out):
    width = out.shape[2]
    for i in range(out.shape[0]):
        out[i] = w_in[:, (i % 2) * width : (i % 2 + 1) * width]


def take_kernel(weights, out):
    out[...] = weights[...]


def pool_kernel(flip, info, slots, ids, rows, out):
    blocks, packed_rows, _ = out.shape
    count = slots.shape[0] // (2 * blocks)
    half = count // 2
    group = packed_rows - half
    blank = jnp.zeros((group, LANES - group * (count // group)), F32)
    side = 1 - info[1] if flip else info[1]

    def step(i, unused):
        at = pl.multiple_of((2 * i + side) * count, count)
        match = jnp.where(slots[pl.ds(at, count), :] == ids[...], 1.0, 0.0).astype(BF)
        part = matmul_t(match, rows[...])
        out[i, 0:half, 0:MAIN] = part[0:half, 0:MAIN].astype(BF)
        out[i, 0:half, MAIN:LANES] = part[half:count, 0:MAIN].astype(BF)
        rest = [part[group * g : group * (g + 1), MAIN:] for g in range(count // group)]
        out[i, half:packed_rows, :] = jnp.concatenate(rest + [blank], axis=1).astype(BF)
        return unused

    lax.fori_loop(0, blocks, step, 0, unroll=4)


def sum_kernel(arrived, out):
    total = jnp.zeros(arrived.shape[1:], F32)
    for i in range(arrived.shape[0]):
        total = total + arrived[i].astype(F32)
    held = total.astype(BF)
    for i in range(out.shape[0]):
        out[i] = held


def embed_kernel(pooled, gain, w_in, out, keep):
    heads, count, size = keep.shape
    each = count // 2
    half = each // 2
    spare = size - MAIN
    group = pooled.shape[1] - half
    square = jnp.zeros((count, 1), F32)
    for h in range(heads):
        two = [pooled[y * heads + h].astype(F32) for y in range(2)]
        main = [v[0:half, at : at + MAIN] for v in two for at in (0, MAIN)]
        main = jnp.concatenate(main, axis=0)
        rest = [v[half:, spare * g : spare * (g + 1)] for v in two for g in range(each // group)]
        rest = jnp.concatenate(rest, axis=0)
        keep[h, :, 0:MAIN] = main
        keep[h, :, MAIN:size] = rest
        square = square + jnp.sum(main * main, axis=1, keepdims=True)
        square = square + jnp.sum(rest * rest, axis=1, keepdims=True)
    scale = lax.rsqrt(square / (heads * size) + EPSILON)
    total = jnp.zeros(out.shape[1:], F32)
    for h in range(heads):
        normed = keep[h] * scale * gain[h : h + 1, :]
        total = total + matmul(normed.astype(BF), w_in[h * size : (h + 1) * size, :])
    held = total.astype(BF)
    for i in range(out.shape[0]):
        out[i] = held


def project_kernel(info, own, other, gain, weights, queries, kv):
    planes = own.shape[0] // 2
    count, width = own.shape[1:]
    size = 2 * width
    columns = 3 * HEAD_SIZE
    square = jnp.zeros((count, width), F32)
    for source in (own, other):
        for b in range(2 * planes):
            wide = source[b].astype(F32)
            square = square + wide * wide
    square = jnp.sum(square, axis=1, keepdims=True)
    scale = lax.rsqrt(square / (2 * planes * size) + EPSILON)
    total = jnp.zeros((count, columns), F32)
    for side, source in ((0, own), (1, other)):
        core = info[0] if side == 0 else 1 - info[0]
        for p in range(planes):
            h = 2 * p + core
            both = jnp.concatenate([source[p], source[planes + p]], axis=1).astype(F32)
            attn_in = both * scale * gain[pl.ds(h, 1), :]
            at = pl.multiple_of(h * size, size)
            total = total + matmul(attn_in.astype(BF), weights[pl.ds(at, size), :])
    queries[...] = total[:, 0:HEAD_SIZE].astype(BF)
    held = total[:, HEAD_SIZE:].astype(BF)
    for i in range(kv.shape[0]):
        kv[i] = held


def attend_kernel(info, queries, slots, labels, *rest):
    pieces, out, scores = rest[:-2], rest[-2], rest[-1]
    query = queries[...]
    own = pl.multiple_of(info[4] * query.shape[0], query.shape[0])
    mine = slots[pl.ds(own, query.shape[0]), :]
    peak = jnp.full((query.shape[0], 1), FLOOR_SCORE, F32)
    turns = ((0, 0), (3, 0), (1, 0), (2, 0), (2, labels.shape[1] // 2))
    start = 0
    for piece, (turn, at) in zip(pieces, turns):
        size = piece.shape[0]
        here = labels[pl.ds((info[3] + turn) % 4, 1), at : at + size]
        part = matmul_t(query, piece[:, 0:HEAD_SIZE]) * (1.0 / math.sqrt(HEAD_SIZE))
        part = jnp.where(here <= mine, part, FLOOR_SCORE)
        scores[:, start : start + size] = part
        peak = jnp.maximum(peak, jnp.max(part, axis=1, keepdims=True))
        start += size
    total = jnp.zeros_like(peak)
    mixed = jnp.zeros(query.shape, F32)
    start = 0
    for piece in pieces:
        size = piece.shape[0]
        weights = jnp.exp(scores[:, start : start + size] - peak)
        total = total + jnp.sum(weights, axis=1, keepdims=True)
        mixed = mixed + matmul(weights.astype(BF), piece[:, HEAD_SIZE:])
        start += size
    out[...] = (mixed / total).astype(BF)


def out_kernel(flip, info, attended, w_out, out):
    count, width = out.shape[1:]
    planes = out.shape[0] // 2
    mine = attended[...]
    at = pl.multiple_of(info[1] * HEAD_SIZE, HEAD_SIZE)
    core = 1 - info[0] if flip else info[0]
    for p in range(planes):
        cols = pl.multiple_of((2 * p + core) * width, width)
        part = matmul(mine, w_out[pl.ds(at, HEAD_SIZE), pl.ds(cols, width)]).astype(BF)
        out[p] = part[0:count]
        out[planes + p] = part[count:]


def down_kernel(info, arrived, embed, w_down, stream, out):
    count, width = stream.shape
    half = count // 2
    planes = embed.shape[0] // 2
    size = MAIN + LONGEST
    at = pl.multiple_of(info[1] * count, count)
    low = embed[info[2], pl.ds(at, count), :]
    high = embed[planes + info[2], pl.ds(at, count), :]
    total = jnp.concatenate([low, high], axis=1).astype(F32)
    added = jnp.zeros(total.shape, F32)
    for h in range(arrived.shape[0]):
        added = added + arrived[h].astype(F32)
    held = (total + added).astype(BF)
    stream[...] = held
    group = out.shape[1] - half
    blank = jnp.zeros((group, LANES - LONGEST * (count // group)), F32)
    for h in range(out.shape[0]):
        part = matmul(held, w_down[h * width : (h + 1) * width, :])
        out[h, 0:half, 0:MAIN] = part[0:half, 0:MAIN].astype(BF)
        out[h, 0:half, MAIN:LANES] = part[half:, 0:MAIN].astype(BF)
        rest = [part[group * g : group * (g + 1), MAIN:size] for g in range(count // group)]
        out[h, half:, :] = jnp.concatenate(rest + [blank], axis=1).astype(BF)


def pick_rows(base, labels_main, labels_rest, states, main, rest, put):
    groups = labels_rest.shape[0]
    half = groups * LONGEST // 2
    for i in range(states.shape[0]):
        main[i * half : (i + 1) * half, :] = states[i, 0:half, :]
        rest[i * LONGEST : (i + 1) * LONGEST, :] = states[i, half:, :]
    step = LANES

    def hot(at, label):
        wanted = base + at + lax.broadcasted_iota(jnp.int32, (step, label.shape[1]), 0)
        return jnp.where(wanted == label, 1.0, 0.0).astype(BF)

    def pick(i, unused):
        at = pl.multiple_of(i * step, step)
        low = matmul(hot(at, labels_main[0:1, :]), main[...])
        high = matmul(hot(at, labels_main[1:2, :]), main[...])
        tail = jnp.zeros((step, LONGEST), F32)
        for g in range(groups):
            here = matmul(hot(at, labels_rest[g : g + 1, :]), rest[...])
            tail = tail + here[:, g * LONGEST : (g + 1) * LONGEST]
        put(at, low[:, 0:MAIN] + high[:, MAIN:LANES], tail)
        return unused

    return pick


def near_kernel(info, spans, labels_main, labels_rest, states, out, main, rest):
    group = info[5]
    out[...] = jnp.zeros(out.shape, F32)

    def put(at, low, tail):
        blank = jnp.zeros((LANES, LANES - MAIN - LONGEST), F32)
        out[pl.ds(at, LANES), :] = jnp.concatenate([low, tail, blank], axis=1)

    pick = pick_rows(
        info[6], labels_main.at[group], labels_rest.at[group], states, main, rest, put
    )
    lax.fori_loop(0, (spans[spans.shape[0] - 1] + LANES - 1) >> 7, pick, 0)


def cross_kernel(
    info, spans, labels_main, labels_rest, ids, rows, states, near, out, picked, main, rest
):
    size = rows.shape[0]
    group = 1 - info[5]
    base = info[6]
    picked[...] = near[...]

    def put(at, low, tail):
        blank = jnp.zeros((LANES, LANES - MAIN - LONGEST), F32)
        here = jnp.concatenate([low, tail, blank], axis=1)
        picked[pl.ds(at, LANES), :] = picked[pl.ds(at, LANES), :] + here

    pick = pick_rows(base, labels_main.at[group], labels_rest.at[group], states, main, rest, put)
    lax.fori_loop(0, (spans[spans.shape[0] - 1] + LANES - 1) >> 7, pick, 0)
    reach = LANES + 2 * WINDOW

    for i in range(rows.shape[1] // LANES):
        at = slice(i * LANES, (i + 1) * LANES)
        mine = rows[:, at]
        start = pl.multiple_of((spans[i] >> 3) << 3, 8)
        keys = picked[pl.ds(start, reach), :].astype(BF)[:, 0:size]
        wanted = base + start + lax.broadcasted_iota(jnp.int32, (reach, LANES), 0)
        far = ids[:, at] - wanted
        close = (far >= 0) & (far < WINDOW) & (wanted >= 0)
        scores = matmul(keys, mine) * (1.0 / math.sqrt(size))
        scores = jnp.where(close, scores, FLOOR_SCORE)
        weights = jnp.exp(scores - jnp.max(scores, axis=0, keepdims=True))
        total = jnp.sum(weights, axis=0, keepdims=True)
        reached = lax.dot_general(
            keys, weights.astype(BF), (((0,), (0,)), ((), ())), preferred_element_type=F32
        )
        out[:, at] = (mine.astype(F32) + reached / total).astype(BF)


def shift(x, axis, by):
    n = lax.axis_size(axis)
    return lax.ppermute(x, axis, [(i, (i + by) % n) for i in range(n)])


def over_plane(copies):
    near = lax.all_to_all(copies, PLANE, 0, 0, tiled=True)
    return near, shift(near, "c", 1)


def over_z(four):
    half = four.shape[0] // 2
    after = shift(four, Z, 1)
    before = shift(four, Z, -1)
    return [four, after, before, shift(four[:half], Z, 2), shift(four[half:], Z, -2)]


def layer(byte_states, patch_ids, slot_patch, pool_gain, w_in, attn_gain, w_qkv, w_out, w_down):
    n_z = lax.axis_size(Z)
    n_zl = lax.axis_size(ZL)
    n_yl = lax.axis_size("yl")
    n_head = lax.axis_size(HEAD)
    patches = slot_patch.shape[0]
    rows_z = patches // n_z
    rows_each = rows_z // n_yl
    bytes_here, cross_size = byte_states.shape
    info = jnp.stack(
        [
            lax.axis_index("c"),
            lax.axis_index("yl"),
            lax.axis_index(("yh", "x")),
            lax.axis_index(ZL),
            lax.axis_index(Z),
            lax.axis_index("zp"),
            patch_ids[0] - (WINDOW - 1),
        ]
    ).astype(jnp.int32)
    n_plane = lax.axis_size(PLANE)
    slots = slot_patch[:, None]
    rows = byte_states.T
    first = info[1] == 0

    w_in_parts = local_call(
        split_kernel,
        jax.ShapeDtypeStruct((n_z * n_yl, w_in.shape[0], w_in.shape[1] // n_yl), BF),
        [w_in],
    )
    w_in_here = lax.all_to_all(w_in_parts, SEQ, 0, 0, tiled=True)
    w_in_here = w_in_here.reshape(-1, w_in_parts.shape[2])

    halves = [
        jnp.concatenate([w_qkv[:, j, k * HEAD_SIZE : (k + 1) * HEAD_SIZE] for j in range(3)], axis=1)
        for k in range(n_yl)
    ]
    depth = w_qkv.shape[0]
    down_pieces = [w_down[:depth], w_down[depth:]]
    sent = jnp.concatenate([jnp.where(first, halves[1], halves[0]), *down_pieces], axis=1)
    came = shift(sent, "yl", 1)
    kept = jnp.concatenate([jnp.where(first, halves[0], halves[1]), *down_pieces], axis=1)
    low = jnp.where(first, kept, came)
    high = jnp.where(first, came, kept)
    wide = halves[0].shape[1]
    part = w_down.shape[1]
    down_both = [
        jnp.concatenate([v[:, wide : wide + part], v[:, wide + part :]], axis=0) for v in (low, high)
    ]
    blank = jnp.zeros((2 * depth, LANES - 2 * part), BF)
    mine = jnp.concatenate([low[:, :wide], high[:, :wide]], axis=0)
    weights = lax.all_gather(
        jnp.concatenate([mine, *down_both, blank], axis=1), Z, axis=0, tiled=True
    )

    packed = jax.ShapeDtypeStruct((n_z, rows_each // 2 + LONGEST, LANES), BF)
    pool_inputs = [info, slots, patch_ids[None, :], rows]
    sent = local_call(functools.partial(pool_kernel, True), packed, pool_inputs, scalars=1)
    came = shift(sent, "yl", 1)
    kept = local_call(functools.partial(pool_kernel, False), packed, pool_inputs, scalars=1)
    pooled = (kept.astype(F32) + came.astype(F32)).astype(BF)
    pooled = lax.all_to_all(pooled, Z, 0, 0, tiled=True)
    pooled = local_call(
        sum_kernel, jax.ShapeDtypeStruct((2 * n_plane, *pooled.shape[1:]), BF), [pooled]
    )
    pooled = lax.all_to_all(pooled, (*PLANE, "c"), 0, 0, tiled=True)
    embed = local_call(
        embed_kernel,
        jax.ShapeDtypeStruct((n_plane, rows_z, w_in_here.shape[1]), BF),
        [pooled, pool_gain.reshape(n_head, cross_size), w_in_here],
        scratch=[pltpu.VMEM((n_head, rows_z, cross_size), F32)],
    )
    own_embed, other_embed = over_plane(embed)
    queries, kv = local_call(
        project_kernel,
        [
            jax.ShapeDtypeStruct((rows_z, HEAD_SIZE), BF),
            jax.ShapeDtypeStruct((n_z // n_zl, rows_z, 2 * HEAD_SIZE), BF),
        ],
        [info, own_embed, other_embed, attn_gain.reshape(n_head, -1), weights],
        scalars=1,
        last=[pl.BlockSpec((weights.shape[0], wide), lambda i: (0, 0))],
    )
    down_here = local_call(
        take_kernel,
        jax.ShapeDtypeStruct((weights.shape[0], LANES), BF),
        [weights],
        last=[pl.BlockSpec((weights.shape[0], LANES), lambda i: (0, wide // LANES))],
    )
    labels = slot_patch.reshape(n_z // n_zl, n_zl, rows_z).transpose(1, 0, 2).reshape(n_zl, -1)
    kv = lax.all_to_all(kv, "zh", 0, 0, tiled=True).reshape(-1, kv.shape[2])
    attended = local_call(
        attend_kernel,
        jax.ShapeDtypeStruct((rows_z, HEAD_SIZE), BF),
        [info, queries, slots, labels, *over_z(kv)],
        scratch=[pltpu.VMEM((rows_z, patches), F32)],
        scalars=1,
    )
    out_shape = jax.ShapeDtypeStruct((n_plane, rows_each, w_out.shape[1] // n_head), BF)
    out_inputs = [info, attended, w_out]
    sent = local_call(functools.partial(out_kernel, True), out_shape, out_inputs, scalars=1)
    came = shift(sent, "c", 1)
    kept = local_call(functools.partial(out_kernel, False), out_shape, out_inputs, scalars=1)
    arrived = lax.all_to_all(
        (kept.astype(F32) + came.astype(F32)).astype(BF), PLANE, 0, 0, tiled=True
    )
    stream, down_part = local_call(
        down_kernel,
        [
            jax.ShapeDtypeStruct((rows_each, w_in.shape[1]), BF),
            jax.ShapeDtypeStruct((n_head, rows_each // 2 + LONGEST, LANES), BF),
        ],
        [info, arrived, own_embed, down_here],
        scalars=1,
    )
    states = lax.all_to_all(down_part, HEAD, 0, 0, tiled=True)
    n_skip = lax.axis_size(SKIP)
    states = local_call(
        sum_kernel, jax.ShapeDtypeStruct((n_skip, *states.shape[1:]), BF), [states]
    )
    states = lax.all_to_all(states, SKIP, 0, 0, tiled=True)
    others = shift(states, "zp", 1)
    by_source = slot_patch.reshape(-1, 2, n_yl, rows_each).transpose(1, 0, 2, 3)
    by_source = by_source.reshape(2, n_skip, rows_each)
    labels_main = by_source.reshape(2, n_skip, 2, -1).transpose(0, 2, 1, 3).reshape(2, 2, -1)
    labels_rest = by_source.reshape(2, n_skip, -1, LONGEST).transpose(0, 2, 1, 3)
    labels_rest = labels_rest.reshape(2, rows_each // LONGEST, -1)
    spans = jnp.concatenate([patch_ids[::LANES], patch_ids[-1:] + WINDOW]) - patch_ids[0]
    capacity = bytes_here + LANES
    room = [
        pltpu.VMEM((n_skip * rows_each // 2, LANES), BF),
        pltpu.VMEM((n_skip * LONGEST, LANES), BF),
    ]
    near = local_call(
        near_kernel,
        jax.ShapeDtypeStruct((capacity, LANES), F32),
        [info, spans, labels_main, labels_rest, states],
        scratch=room,
        scalars=2,
    )
    byte_out = local_call(
        cross_kernel,
        jax.ShapeDtypeStruct((cross_size, bytes_here), BF),
        [info, spans, labels_main, labels_rest, patch_ids[None, :], rows, others, near],
        scratch=[pltpu.VMEM((capacity, LANES), F32), *room],
        scalars=2,
    ).T
    return (stream, byte_out)


def solution(mesh):
    torus = Mesh(
        mesh.devices.reshape(4, 2, 2, 2, 2, 4, 2), ("zh", "zm", "zp", "yl", "yh", "x", "c")
    )
    return jax.shard_map(
        layer,
        mesh=torus,
        in_specs=(
            P(SEQ, HEAD),
            P(SEQ),
            P(),
            P(),
            P(SEQ, HEAD),
            P(),
            P(SEQ, None, HEAD),
            P(HEAD, None),
            P(HEAD, SEQ),
        ),
        out_specs=(P(SEQ, HEAD), P(SEQ, HEAD)),
        check_vma=False,
    )
```
